256 devices in a mesh: box: 64 (over y, z, core), rank: 4 (over x).
Axes of the slice: x: 4, y: 4, z: 8, core: 2. Of those that a mesh axis runs over, the one named last changes fastest.
Arguments:
- coeffs: float32 [1000, 16384], P(None, 'box'), may hold values from -6 to 6
- operator: float32 [12, 3, 3, 10, 10], P('rank'), may hold values from -1 to 1
- filters: float32 [2, 10, 10], replicated, may hold values from -2 to 2
- neighbours: int32 [7, 16384], P(None, 'box'), may hold values from -1 to 16383, as said below
- parent_one: int32 [16384], P('box'), may hold values from -1 to 2047, as said below
- octant_one: int32 [16384], P('box'), may hold values from 0 to 7, as said below
- parent_two: int32 [2048], P('box'), may hold values from -1 to 255, as said below
- octant_two: int32 [2048], P('box'), may hold values from 0 to 7, as said below
- keep: int32 [16384], P('box'), may hold values 0 or 1
Outputs:
- leaves: float32 [1000, 16384], P(None, 'box')
- level_one: float32 [1000, 2048], P(None, 'box')
- level_two: float32 [1000, 256], P(None, 'box')
The draws below stay inside these ranges and needn't reach their ends.
Inputs may be any that keep to these rules, and one draw needn't show every extreme that they name: Leaf boxes tile 160 cubes of 4 x 4 x 4 laid along x, in Morton order within each cube and cube after cube; each index of box holds a contiguous run of them in its first slots, between 64 and 256 boxes, and some index holds 256. neighbours[e, s] is the slot of the face neighbour of the box in slot s at displacement e, -1 where slot s is empty or the neighbour lies outside the domain; a neighbour on another index lies on the next one within its first 64 slots, or on the previous one within its last 64 occupied slots. `parent_one`: A parent is held by the index of box that holds its first child, in the order of its parents; only the first seven leaves of an index can have a parent on another index, and then it is the last parent of the previous index. -1 marks empty slots. `octant_one`: bits 0, 1, 2 tell whether the box is the upper child along x, y, z; 0 in empty slots. `parent_two`: likewise one level up: only the first seven level-one boxes of an index can have a parent on another index, and then it is the last parent of the previous index. -1 marks empty slots. `octant_two`: bits 0, 1, 2 tell whether the box is the upper child along x, y, z; 0 in empty slots.
All inputs are finite; a program needn't handle non-finite values. No bound on the sum of `keep` on one device may be relied on, other than what follows from the above.
Results may differ from the reference program's by a relative error of at most 0.00013.
Values sent between devices are 32-bit elements; how exact they have to be, the bound alone decides.
No kernel may reach another device: no remote copies, remote signals or barrier semaphores. Data moves between devices by JAX's collectives and lax.ppermute only.
A program may use at most 128 MiB of HBM per device.

```python
import jax
import jax.numpy as jnp
from jax import lax

K = 10
KKK = 1000
RANK = 12
CAP = 256
MEAN = 160
BOXES = 16384
NCUBE = 160


SHIFT_STEPS = ((0, 0, 0), (-1, 0, 0), (1, 0, 0), (0, -1, 0), (0, 1, 0), (0, 0, -1), (0, 0, 1))


def encode_cell(along_x, along_y, along_z):
    return along_x % 2 + 2 * (along_y % 2) + 4 * (along_z % 2) + 8 * (along_x // 2) + 16 * (along_y // 2) + 32 * (along_z // 2)


def owner_of(morton, starts):
    return jnp.sum((starts[None, :] <= morton[:, None]).astype(jnp.int32), axis=1) - 1


def tree_layout(key):
    device_total = BOXES // CAP
    base_key = jax.random.fold_in(key, 9173)
    pick_key, weight_key = jax.random.split(base_key)
    special = jax.random.randint(pick_key, (), 0, device_total)
    device_ids = jnp.arange(device_total)
    weights = jax.random.randint(weight_key, (device_total,), 4096, 8192)
    weights = jnp.where(device_ids == special, 0, weights)
    spread_total = (MEAN - CAP // 4) * device_total - (CAP - CAP // 4)
    extras = weights * spread_total // jnp.sum(weights)
    leftover = spread_total - jnp.sum(extras)
    others = (device_ids != special).astype(jnp.int32)
    rank_other = jnp.cumsum(others) - 1
    extras = extras + others * (rank_other < leftover).astype(jnp.int32)
    counts = jnp.where(device_ids == special, CAP, CAP // 4 + extras)
    starts = jnp.cumsum(counts) - counts
    slot_ids = jnp.arange(BOXES)
    holder = slot_ids // CAP
    within = slot_ids % CAP
    is_live = within < counts[holder]
    morton = jnp.where(is_live, starts[holder] + within, 0)
    cube_index = morton // 64
    inner_index = morton % 64
    cell_x = 4 * cube_index + inner_index % 2 + 2 * (inner_index // 8 % 2)
    cell_y = inner_index // 2 % 2 + 2 * (inner_index // 16 % 2)
    cell_z = inner_index // 4 % 2 + 2 * (inner_index // 32 % 2)
    listed = []
    for shift_x, shift_y, shift_z in SHIFT_STEPS:
        next_x = cell_x + shift_x
        next_y = cell_y + shift_y
        next_z = cell_z + shift_z
        inside = (next_x >= 0) & (next_x < 4 * NCUBE) & (next_y >= 0) & (next_y < 4) & (next_z >= 0) & (next_z < 4)
        clip_x = jnp.clip(next_x, 0, 4 * NCUBE - 1)
        clip_y = jnp.clip(next_y, 0, 3)
        clip_z = jnp.clip(next_z, 0, 3)
        target = clip_x // 4 * 64 + encode_cell(clip_x % 4, clip_y, clip_z)
        owner_box = owner_of(target, starts)
        slot_index = owner_box * CAP + target - starts[owner_box]
        listed.append(jnp.where(is_live & inside, slot_index, -1))
    neighbours = jnp.stack(listed).astype(jnp.int32)
    first_one = (starts + 7) // 8
    parent_index = morton // 8
    owner_one = owner_of(parent_index * 8, starts)
    parent_one = jnp.where(is_live, owner_one * (CAP // 8) + parent_index - first_one[owner_one], -1)
    octant_one = jnp.where(is_live, morton % 8, 0)
    level_slots = jnp.arange(BOXES // 8)
    holder_one = level_slots // (CAP // 8)
    within_one = level_slots % (CAP // 8)
    ends_one = (starts + counts + 7) // 8
    live_one = within_one < (ends_one - first_one)[holder_one]
    box_one = jnp.where(live_one, first_one[holder_one] + within_one, 0)
    first_two = (starts + 63) // 64
    grand_index = box_one // 8
    owner_two = owner_of(grand_index * 64, starts)
    parent_two = jnp.where(live_one, owner_two * (CAP // 64) + grand_index - first_two[owner_two], -1)
    octant_two = jnp.where(live_one, box_one % 8, 0)
    return (neighbours, parent_one.astype(jnp.int32), octant_one.astype(jnp.int32), parent_two.astype(jnp.int32), octant_two.astype(jnp.int32))


def draw_neighbours(key, part):
    return tree_layout(key)[0]


def draw_parent_one(key, part):
    return tree_layout(key)[1]


def draw_octant_one(key, part):
    return tree_layout(key)[2]


def draw_parent_two(key, part):
    return tree_layout(key)[3]


def draw_octant_two(key, part):
    return tree_layout(key)[4]


def with_ends(array, stream_key, smallest, high):
    extent = array.shape
    spot = [jax.random.randint(jax.random.fold_in(stream_key, axis), (), 0, extent[axis]) for axis in range(len(extent))]
    array = array.at[tuple(spot)].set(smallest)
    longest = extent.index(max(extent))
    spot[longest] = (spot[longest] + 1) % extent[longest]
    return array.at[tuple(spot)].set(high)


def block_levels(own_key, extent, cuts, smallest, top_value):
    gain, own = 1.0, jax.random.fold_in(own_key, 6)
    for position, blocks in cuts:
        heights = jnp.exp(jax.random.uniform(jax.random.fold_in(own, position), (blocks,), jnp.float32, smallest / len(cuts), top_value / len(cuts)))
        gain = gain * jnp.repeat(heights, extent[position] // blocks).reshape([-1 if axis == position else 1 for axis in range(len(extent))])
    return gain


def scatter_about(own_key, shape, deviation, most, shards=(), held_as=jnp.bfloat16):
    values = jax.random.normal(own_key, shape, jnp.float32) * deviation
    if len(shards) > 0:
        values = block_levels(own_key, shape, shards, -0.22, 0.18) * values
    return jnp.clip(values, min=-most, max=most).astype(held_as)


def setup_inputs(seed: int = 0) -> dict:
    key_of = jax.random.split(jax.random.key(seed), 10)
    coeffs = scatter_about(key_of[0], (KKK, BOXES), 1.0, 6.0, ((1, 64),), jnp.float32)
    operator = scatter_about(key_of[1], (RANK, 3, 3, K, K), (4 * K) ** -0.5, 1.0, ((0, 4),), jnp.float32)
    filters = scatter_about(key_of[2], (2, K, K), K ** -0.5, 2.0, (), jnp.float32)
    neighbours = draw_neighbours(jax.random.fold_in(key_of[9], 71), 0)
    parent_one = draw_parent_one(jax.random.fold_in(key_of[9], 71), 0)
    octant_one = draw_octant_one(jax.random.fold_in(key_of[9], 71), 0)
    parent_two = draw_parent_two(jax.random.fold_in(key_of[9], 71), 0)
    octant_two = draw_octant_two(jax.random.fold_in(key_of[9], 71), 0)
    keep = with_ends((jax.random.randint(key_of[8], (BOXES,), 0, 4) < 3).astype(jnp.int32), jax.random.fold_in(key_of[8], 1), 0, 1)
    return dict(coeffs=coeffs, operator=operator, filters=filters, neighbours=neighbours, parent_one=parent_one, octant_one=octant_one, parent_two=parent_two, octant_two=octant_two, keep=keep)


SHIFT_CODES = ((0, 0, 0), (1, 0, 0), (2, 0, 0), (0, 1, 0), (0, 2, 0), (0, 0, 1), (0, 0, 2))
HIGHEST_MODE = lax.Precision.HIGHEST
CHILD_SCALE = 8.0 ** -0.5


def apply_terms(factors, source, basis_order):
    box_count = source.shape[1]
    tensor = source.reshape(basis_order, basis_order, basis_order, box_count)
    step_one = jnp.einsum('rai,ijkn->rajkn', factors[:, 0], tensor, precision=HIGHEST_MODE)
    step_two = jnp.einsum('rbj,rajkn->rabkn', factors[:, 1], step_one, precision=HIGHEST_MODE)
    step_three = jnp.einsum('rck,rabkn->abcn', factors[:, 2], step_two, precision=HIGHEST_MODE)
    return step_three.reshape(basis_order ** 3, box_count)


def child_filter(values, octants, filters, basis_order):
    box_count = values.shape[1]
    tensor = values.reshape(basis_order, basis_order, basis_order, box_count)
    low_bit = (octants % 2)[None, None, None, :] == 1
    mid_bit = ((octants // 2) % 2)[None, None, None, :] == 1
    top_bit = (octants // 4)[None, None, None, :] == 1
    lower = jnp.einsum('ai,ijkn->ajkn', filters[0], tensor, precision=HIGHEST_MODE)
    upper = jnp.einsum('ai,ijkn->ajkn', filters[1], tensor, precision=HIGHEST_MODE)
    tensor = jnp.where(low_bit, upper, lower)
    lower = jnp.einsum('bj,ijkn->ibkn', filters[0], tensor, precision=HIGHEST_MODE)
    upper = jnp.einsum('bj,ijkn->ibkn', filters[1], tensor, precision=HIGHEST_MODE)
    tensor = jnp.where(mid_bit, upper, lower)
    lower = jnp.einsum('ck,ijkn->ijcn', filters[0], tensor, precision=HIGHEST_MODE)
    upper = jnp.einsum('ck,ijkn->ijcn', filters[1], tensor, precision=HIGHEST_MODE)
    tensor = jnp.where(top_bit, upper, lower)
    return tensor.reshape(basis_order ** 3, box_count) * CHILD_SCALE


def gather_level(terms, parents, slot_total):
    safe_ids = jnp.where(parents >= 0, parents, slot_total).astype(jnp.int32)
    summed = jax.ops.segment_sum(terms.T, safe_ids, num_segments=slot_total + 1)
    return summed[:slot_total].T


def reference(coeffs, operator, filters, neighbours, parent_one, octant_one, parent_two, octant_two, keep):
    basis_order = filters.shape[1]
    applied = jnp.zeros(coeffs.shape, jnp.float32)
    for displacement in range(len(SHIFT_CODES)):
        shift_code = SHIFT_CODES[displacement]
        present = (neighbours[displacement] >= 0).astype(jnp.float32)
        picked = jnp.maximum(neighbours[displacement], 0).astype(jnp.int32)
        source = jnp.take(coeffs, picked, axis=1) * present[None, :]

        def add_term(rank_term, summed):
            factors = jnp.stack([operator[rank_term, 0, shift_code[0]], operator[rank_term, 1, shift_code[1]], operator[rank_term, 2, shift_code[2]]])[None]
            return summed + apply_terms(factors, source, basis_order)

        applied = lax.fori_loop(0, RANK, add_term, applied)
    level_total = parent_two.shape[0]
    level_one = gather_level(child_filter(applied, octant_one, filters, basis_order), parent_one, level_total)
    level_two = gather_level(child_filter(level_one, octant_two, filters, basis_order), parent_two, level_total // 8)
    return applied * keep[None, :].astype(jnp.float32), level_one, level_two
```

```python
import jax
import jax.numpy as jnp
import numpy as np
from jax import lax
from jax.experimental import pallas as pl
from jax.experimental.pallas import tpu as pltpu
from jax.sharding import PartitionSpec as P

F32 = jnp.float32
BF16 = jnp.bfloat16
I32 = jnp.int32
HIGHEST_MODE = lax.Precision.HIGHEST
CHILD_SCALE = 8.0 ** (-0.5)

K = 10
SQ = 100
KKK = 1000
CAP = 256
EDGE = 64
HALF = 504
LANES = 128
KT = 60
MROWS = 1008
GROUPS = 6

SAME_X = (0, 3, 4, 5, 6)
Y_CODE = {0: 0, 3: 1, 4: 2, 5: 0, 6: 0}
Z_CODE = {0: 0, 3: 0, 4: 0, 5: 1, 6: 2}


def split(value):
    high = value.astype(BF16)
    low = (value - high.astype(F32)).astype(BF16)
    return high, low


def mm(a, b):
    return jnp.dot(a, b, preferred_element_type=F32)


def mm_t(a, b):
    return lax.dot_general(a, b, (((1,), (1,)), ((), ())), preferred_element_type=F32)


def mm_full(a, b):
    return jnp.dot(a, b, preferred_element_type=F32, precision=HIGHEST_MODE)


def iota(shape, dim):
    return lax.broadcasted_iota(I32, shape, dim)


def tenth(index):
    return jnp.floor((index.astype(F32) + 0.5) * 0.1).astype(I32)


def edges_kernel(x_ref, nb_ref, head_ref, tail_ref):
    count = jnp.sum((nb_ref[0:1, :] >= 0).astype(F32), axis=1, keepdims=True)
    row = iota((2 * CAP, 2 * LANES), 0)
    lane = iota((2 * CAP, 2 * LANES), 1)
    slot = row & (CAP - 1)
    same_half = (row >= CAP) == ((lane & (LANES - 1)) >= EDGE)
    column = lane & (EDGE - 1)
    wanted = jnp.where(lane < LANES, column, column - EDGE + count.astype(I32))
    pick = ((slot == wanted) & same_half).astype(F32).astype(BF16)
    top_high, top_low = split(x_ref[0:HALF, :])
    below = jnp.concatenate([x_ref[HALF:KKK, :], jnp.zeros((2 * HALF - KKK, CAP), F32)], axis=0)
    low_high, low_low = split(below)
    both = mm(top_high, pick[:CAP]) + mm(top_low, pick[:CAP])
    both = both + (mm(low_high, pick[CAP:]) + mm(low_low, pick[CAP:]))
    head_ref[...] = both[:, :LANES]
    spot = (iota((HALF, LANES), 0) == HALF - 1) & (iota((HALF, LANES), 1) >= EDGE)
    tail_ref[...] = jnp.where(spot, count, both[:, LANES:])


def compress(value_ref, select, ff_high, ff_low, filter_smem, work_ref, out_ref):
    high, low = split(value_ref[0:KKK, :])
    span = KKK + 32
    for w in range(4):
        part = select[w * LANES : (w + 1) * LANES]
        work_ref[w * span : w * span + KKK, :] = mm_t(high, part) + mm_t(low, part)
        work_ref[w * span + KKK : (w + 1) * span, :] = jnp.zeros((32, LANES), F32)
    base = 4 * span
    for pair in range(5):
        columns = []
        for i in (2 * pair, 2 * pair + 1):
            columns.append(
                jnp.concatenate(
                    [work_ref[w * span + i * SQ : w * span + i * SQ + LANES, :] for w in range(4)],
                    axis=0,
                )
            )
        rhs_high, rhs_low = split(jnp.concatenate(columns, axis=1))
        z = mm(ff_high, rhs_high) + mm(ff_low, rhs_high) + mm(ff_high, rhs_low)
        work_ref[base + 208 * pair : base + 208 * pair + 104, :] = z[:, :LANES]
        work_ref[base + 208 * pair + 104 : base + 208 * pair + 208, :] = z[:, LANES:]
    upper = iota((1, LANES), 1) >= 64
    for a in range(K):
        total = None
        for i in range(K):
            weight = jnp.where(upper, filter_smem[1, a, i], filter_smem[0, a, i]) * CHILD_SCALE
            term = work_ref[base + 104 * i : base + 104 * i + 104, :] * weight
            total = term if total is None else total + term
        total = total + pltpu.roll(total, 64, axis=1)
        out_ref[a * SQ : (a + 1) * SQ, :] = total[:SQ]


def main_kernel(
    x_ref,
    left_ref,
    right_ref,
    op0_ref,
    op1_ref,
    op2_ref,
    op3_ref,
    ints_ref,
    cols_ref,
    filter_ref,
    filter_smem,
    leaves_ref,
    one_ref,
    two_ref,
    send_ref,
    w_high,
    w_low,
    stage,
    s_high,
    s_low,
    s_stage,
    x_pad,
    edge,
    picks,
    b_wide,
    c_wide,
    ops,
    acc_ref,
    applied,
    level,
    level_up,
):
    ops[...] = jnp.zeros_like(ops)
    for n, ref in enumerate((op0_ref, op1_ref, op2_ref, op3_ref)):
        ops[3 * n : 3 * n + 3, 0:900] = ref[...]
    factors = ops[...]
    row = iota((104, LANES), 0)
    lane = iota((104, LANES), 1)
    spread = jnp.where(row < 80, (row >> 3) * 10 + (row & 7), 0)
    spread = jnp.where((row >= 80) & (row < 88), (row - 80) * 10 + 8, spread)
    spread = jnp.where((row >= 88) & (row < 96), (row - 88) * 10 + 9, spread)
    spread = jnp.where(row >= 96, 80 + ((row - 96) >> 1) * 10 + 8 + (row & 1), spread)
    order = ((spread == lane) & (row < 100)).astype(F32).astype(BF16)
    x_factor = []
    for code in range(3):
        moved = factors if code == 0 else pltpu.roll(factors, 1024 - SQ * code, axis=1)
        high, low = split(moved[:, :LANES])
        x_factor.append(mm_t(order, jnp.concatenate([high, low, high], axis=0)).astype(BF16))
    x_same = x_factor[0]
    x_moved = jnp.concatenate([x_factor[1], x_factor[2]], axis=0)
    column_of = iota((384, 512), 0)
    y_cols = (column_of == cols_ref[0:1, :]).astype(F32)
    z_cols = (column_of == cols_ref[1:2, :]).astype(F32)
    y_rows = [pltpu.roll(factors, 1024 - 300 - 10 * b, axis=1)[:, :384] for b in range(K)]
    z_rows = [pltpu.roll(factors, 1024 - 600 - 10 * b, axis=1)[:, :384] for b in range(K)]
    b_wide[...] = mm_full(jnp.concatenate(y_rows, axis=0), y_cols).reshape(K, 16, 512)
    c_wide[...] = mm_full(jnp.concatenate(z_rows, axis=0), z_cols).reshape(K, 16, 512)

    def build(pair_of, count, width):
        step = width // K if width == 160 else 4

        def put(value, first_tile, position, tiles):
            for l in range(tiles):
                t = first_tile + l
                part = value[:, l * LANES : (l + 1) * LANES]
                for a in range(K):
                    stage[pl.ds(t * width + a * step + position, 8, stride=6 * width), :] = part[
                        8 * a : 8 * a + 8
                    ]
                for n, i in enumerate((8, 9)):
                    stage[
                        pl.ds((i * 6 + t) * width + position, 8, stride=step), :
                    ] = part[80 + 8 * n : 88 + 8 * n]
                for n, a in enumerate((8, 9)):
                    stage[
                        pl.ds((48 + t) * width + a * step + position, 2, stride=6 * width), :
                    ] = part[96 + 2 * n : 98 + 2 * n]

        held = []
        for u in range(count):
            b, c = pair_of(u)
            high, low = split(b_wide[b] * c_wide[c])
            rhs = jnp.concatenate([high, high, low], axis=0)
            for half in range(2):
                put(mm(x_same, rhs[:, 256 * half : 256 * half + 256]), 2 * half, u, 2)
            held.append(rhs[:, :LANES])
            if len(held) == 2:
                both = mm(x_moved, jnp.concatenate(held, axis=1))
                for n in range(2):
                    put(both[:104, n * LANES : (n + 1) * LANES], 4, u - 1 + n, 1)
                    put(both[104:, n * LANES : (n + 1) * LANES], 5, u - 1 + n, 1)
                held = []

    def one_group(g, carry):
        def pair_of(u):
            p = g * 16 + u
            b = (p * 205) >> 11
            return b, p - 10 * b

        build(pair_of, 16, 160)
        first = pl.multiple_of(g * 160, 160)
        for t in range(KT):
            high, low = split(stage[t * 160 : (t + 1) * 160, :])
            w_high[pl.ds(first, 160), t * LANES : (t + 1) * LANES] = high
            w_low[pl.ds(first, 160), t * LANES : (t + 1) * LANES] = low
        return carry

    lax.fori_loop(0, GROUPS, one_group, 0)
    stage[0 : KT * 48, :] = jnp.zeros((KT * 48, LANES), F32)
    build(lambda u: (9, 6 + u), 4, 48)
    for t in range(KT):
        high, low = split(stage[t * 48 : (t + 1) * 48, :])
        w_high[960:MROWS, t * LANES : (t + 1) * LANES] = high
        w_low[960:MROWS, t * LANES : (t + 1) * LANES] = low

    first_half = iota((HALF, LANES), 1) < EDGE
    left = left_ref[...]
    right = right_ref[...]
    edge[0:HALF, :] = jnp.where(first_half, left, pltpu.roll(right, EDGE, axis=1))
    edge[HALF : 2 * HALF, :] = jnp.where(first_half, pltpu.roll(left, EDGE, axis=1), right)
    for i in range(K):
        x_pad[112 * i : 112 * i + SQ, 0:CAP] = x_ref[SQ * i : SQ * i + SQ, :]
        x_pad[112 * i : 112 * i + SQ, CAP : CAP + LANES] = edge[SQ * i : SQ * i + SQ, :]
        x_pad[112 * i + SQ : 112 * i + 112, :] = jnp.zeros((12, CAP + LANES), F32)
    near = ints_ref[0:8, :]
    origin = near[0:1, 0:1]
    before = left[HALF - 1 : HALF, EDGE : EDGE + 1].astype(I32)
    moved = near - origin
    place = jnp.where(moved < 0, moved + (2 * CAP + EDGE) - before, moved)
    place = jnp.where(moved >= CAP, moved + EDGE, place)
    place = jnp.where(near >= 0, place, -1)
    live = (near[0:1, :] >= 0).astype(F32)
    slots = iota((CAP + LANES, CAP), 0)
    for e in range(1, 7):
        picks[e - 1] = (slots == place[e : e + 1, :]).astype(F32).astype(BF16)
    s_stage[500:512, :] = jnp.zeros((12, CAP), F32)
    s_stage[612:640, :] = jnp.zeros((28, CAP), F32)
    s_stage[740:768, :] = jnp.zeros((28, CAP), F32)

    def one_i(i, carry):
        rows = x_pad[pl.ds(pl.multiple_of(i * 112, 112), 112), :]
        high, low = split(rows)
        wide = jnp.concatenate(
            [high[:, :CAP], low[:, :CAP], high[:, CAP:], low[:, CAP:]], axis=1
        )
        s_stage[0:SQ, :] = rows[:SQ, :CAP] * live
        for e in range(1, 7):
            pick = picks[e - 1]
            near_pick = pick[:CAP]
            far_pick = pick[CAP:]
            taken = mm(
                wide, jnp.concatenate([near_pick, near_pick, far_pick, far_pick], axis=0)
            )
            at = 512 if e == 1 else 640 if e == 2 else SQ * (e - 2)
            s_stage[at : at + SQ, :] = taken[:SQ]
        high, low = split(s_stage[...])
        at = pl.multiple_of(i * 768, 768)
        s_high[pl.ds(at, 768), :] = high
        s_low[pl.ds(at, 768), :] = low
        return carry

    lax.fori_loop(0, K, one_i, 0)

    acc_ref[...] = mm(w_high[...], s_high[...])
    acc_ref[...] += mm(w_low[...], s_high[...])
    acc_ref[...] += mm(w_high[...], s_low[...])
    for a in range(K):
        for g in range(GROUPS):
            applied[a * SQ + 16 * g : a * SQ + 16 * g + 16, :] = acc_ref[
                g * 160 + a * 16 : g * 160 + a * 16 + 16, :
            ]
        applied[a * SQ + 96 : a * SQ + SQ, :] = acc_ref[960 + 4 * a : 964 + 4 * a, :]
    leaves_ref[...] = applied[...] * ints_ref[10:11, :].astype(F32)

    p_row = iota((104, 16), 0)
    small = iota((104, 16), 1)
    b_of = tenth(p_row)
    c_of = p_row - 10 * b_of
    pick_b = ((b_of == small) & (p_row < SQ)).astype(F32)
    pick_c = ((c_of == small) & (p_row < SQ)).astype(F32)
    q_lane = iota((16, LANES), 1)
    j_of = tenth(q_lane)
    k_of = q_lane - 10 * j_of
    small = iota((16, LANES), 0)
    pick_j = ((j_of == small) & (q_lane < SQ)).astype(F32)
    pick_k = ((k_of == small) & (q_lane < SQ)).astype(F32)
    y_filter = []
    z_filter = []
    for f in range(2):
        level_up[0:16, :] = jnp.zeros((16, LANES), F32)
        level_up[0:K, 0:K] = filter_ref[f]
        square = level_up[0:16, :]
        left_b = mm_full(pick_b, square)
        left_c = mm_full(pick_c, square)
        grown = jnp.zeros((112, LANES), F32)
        wide_j = jnp.concatenate([pick_j, grown], axis=0)
        wide_k = jnp.concatenate([pick_k, grown], axis=0)
        y_filter.append(mm_full(left_b, wide_j))
        z_filter.append(mm_full(left_c, wide_k))
    ff = jnp.concatenate(
        [y_filter[0] * z_filter[0], y_filter[1] * z_filter[0], y_filter[0] * z_filter[1], y_filter[1] * z_filter[1]],
        axis=1,
    )
    ff_high, ff_low = split(ff)
    parent = ints_ref[8:9, :]
    octant = ints_ref[9:10, :]
    local = parent - (origin >> 3)
    local = jnp.where(local < 0, 32, local)
    code = (octant >> 1) * LANES + (octant & 1) * 64 + local
    code = jnp.where(parent >= 0, code, -1)
    rows = iota((4 * LANES, CAP), 0)
    select = (rows == code).astype(F32).astype(BF16)
    compress(applied, select, ff_high, ff_low, filter_smem, stage, level)
    parent = ints_ref[11:12, 0:LANES]
    octant = ints_ref[12:13, 0:LANES]
    lane = iota((1, LANES), 1)
    local = parent - (origin >> 6)
    local = jnp.where(local < 0, 4, local)
    code = (octant >> 1) * LANES + (octant & 1) * 64 + local
    code = jnp.where((parent >= 0) & (lane < 32), code, -1)
    last = (octant[:, 0:1] + 7) & 7
    code = jnp.where(lane == 32, (last >> 1) * LANES + (last & 1) * 64 + 4, code)
    rows = iota((4 * LANES, LANES), 0)
    select = (rows == code).astype(F32).astype(BF16)
    compress(level, select, ff_high, ff_low, filter_smem, stage, level_up)
    one_ref[...] = level[:, 0:32]
    two_ref[...] = level_up[:, 0:4]
    row = iota((8, LANES), 0)
    lane = iota((8, LANES), 1)
    pick_one = ((row == 0) & (lane == 32)).astype(F32)
    pick_two = ((row == 1) & (lane == 4)).astype(F32)
    sent = lax.dot_general(
        pick_one, level[...], (((1,), (1,)), ((), ())), preferred_element_type=F32, precision=HIGHEST_MODE
    ) + lax.dot_general(
        pick_two, level_up[...], (((1,), (1,)), ((), ())), preferred_element_type=F32, precision=HIGHEST_MODE
    )
    send_ref[...] = sent


def column_table():
    table = np.full((8, 512), -1, np.int32)
    for n, e in enumerate(SAME_X):
        for j in range(K):
            for k in range(K):
                at = n * SQ + j * K + k
                table[0, at] = Y_CODE[e] * SQ + j
                table[1, at] = Z_CODE[e] * SQ + k
    return table


VMEM_SPEC = pl.BlockSpec(memory_space=pltpu.VMEM)
SMEM_SPEC = pl.BlockSpec(memory_space=pltpu.SMEM)
PARAMS = pltpu.CompilerParams(vmem_limit_bytes=63 * 1024 * 1024)


def shape(dims, dtype=F32):
    return jax.ShapeDtypeStruct(dims, dtype)


def edges(coeffs, neighbours):
    return pl.pallas_call(
        edges_kernel,
        out_shape=(shape((HALF, LANES)), shape((HALF, LANES))),
        in_specs=[VMEM_SPEC] * 2,
        out_specs=(VMEM_SPEC,) * 2,
        name="edges",
    )(coeffs, neighbours)


def gather_ints(neighbours, parent_one, octant_one, parent_two, octant_two, keep):
    wide = lambda v: jnp.pad(v, (0, CAP - v.shape[0]))[None]
    blank = jnp.full((1, CAP), -1, I32)
    rows = [neighbours, blank, parent_one[None], octant_one[None], keep[None]]
    rows += [wide(parent_two), wide(octant_two), blank, blank, blank]
    return jnp.concatenate(rows, axis=0)


def operator_step(coeffs, from_left, from_right, terms, ints, filters):
    return pl.pallas_call(
        main_kernel,
        out_shape=(shape((KKK, CAP)), shape((KKK, 32)), shape((KKK, 4)), shape((8, KKK))),
        in_specs=[VMEM_SPEC] * 10 + [SMEM_SPEC],
        out_specs=(VMEM_SPEC,) * 4,
        scratch_shapes=[
            pltpu.VMEM((MROWS, KT * LANES), BF16),
            pltpu.VMEM((MROWS, KT * LANES), BF16),
            pltpu.VMEM((KT * 160, LANES), F32),
            pltpu.VMEM((KT * LANES, CAP), BF16),
            pltpu.VMEM((KT * LANES, CAP), BF16),
            pltpu.VMEM((768, CAP), F32),
            pltpu.VMEM((1120, CAP + LANES), F32),
            pltpu.VMEM((2 * HALF, LANES), F32),
            pltpu.VMEM((6, CAP + LANES, CAP), BF16),
            pltpu.VMEM((K, 16, 512), F32),
            pltpu.VMEM((K, 16, 512), F32),
            pltpu.VMEM((16, 1024), F32),
            pltpu.VMEM((MROWS, CAP), F32),
            pltpu.VMEM((KKK, CAP), F32),
            pltpu.VMEM((KKK, LANES), F32),
            pltpu.VMEM((KKK, LANES), F32),
        ],
        compiler_params=PARAMS,
        name="operator",
    )(coeffs, from_left, from_right, *terms, ints, jnp.asarray(column_table()), filters, filters)


def per_device(
    coeffs, operator, filters, neighbours, parent_one, octant_one, parent_two, octant_two, keep
):
    terms = operator.reshape(3, 900)
    others = [
        lax.ppermute(terms, "rank", [(i, (i + step) % 4) for i in range(4)]) for step in (1, 2, 3)
    ]
    head, tail = edges(coeffs, neighbours)
    count = lax.axis_size("box")
    from_left = lax.ppermute(tail, "box", [(i, i + 1) for i in range(count - 1)])
    from_right = lax.ppermute(head, "box", [(i + 1, i) for i in range(count - 1)])
    ints = gather_ints(neighbours, parent_one, octant_one, parent_two, octant_two, keep)
    leaves, level_one, level_two, sent = operator_step(
        coeffs, from_left, from_right, (terms, *others), ints, filters
    )
    received = lax.ppermute(sent[:2], "box", [(i + 1, i) for i in range(count - 1)])
    me = lax.axis_index("box")
    slots_one = jnp.arange(level_one.shape[1])
    slots_two = jnp.arange(level_two.shape[1])
    last_one = jnp.max(parent_one) - me * level_one.shape[1]
    last_two = jnp.max(parent_two) - me * level_two.shape[1]
    level_one = level_one + received[0][:, None] * (slots_one == last_one)[None, :].astype(F32)
    level_two = level_two + received[1][:, None] * (slots_two == last_two)[None, :].astype(F32)
    return leaves, level_one, level_two


def solution(mesh):
    placed = (
        P(None, "box"),
        P("rank", None, None, None, None),
        P(),
        P(None, "box"),
        P("box"),
        P("box"),
        P("box"),
        P("box"),
        P("box"),
    )
    return jax.shard_map(
        per_device,
        mesh=mesh,
        in_specs=placed,
        out_specs=(P(None, "box"), P(None, "box"), P(None, "box")),
        check_vma=False,
    )
```

```python
import jax
import jax.numpy as jnp
import numpy as np
from jax import lax
from jax.experimental import pallas as pl
from jax.experimental.pallas import tpu as pltpu
from jax.sharding import PartitionSpec as P

F32 = jnp.float32
BF16 = jnp.bfloat16
I32 = jnp.int32
HIGHEST_MODE = lax.Precision.HIGHEST
CHILD_SCALE = 8.0 ** (-0.5)

K = 10
SQ = 100
KKK = 1000
CAP = 256
EDGE = 64
HALF = 504
LANES = 128
KT = 60
MROWS = 1008
GROUPS = 6

SAME_X = (0, 3, 4, 5, 6)
Y_CODE = {0: 0, 3: 1, 4: 2, 5: 0, 6: 0}
Z_CODE = {0: 0, 3: 0, 4: 0, 5: 1, 6: 2}


def split(value):
    high = value.astype(BF16)
    low = (value - high.astype(F32)).astype(BF16)
    return high, low


def mm(a, b):
    return jnp.dot(a, b, preferred_element_type=F32)


def mm_t(a, b):
    return lax.dot_general(a, b, (((1,), (1,)), ((), ())), preferred_element_type=F32)


def mm_full(a, b):
    return jnp.dot(a, b, preferred_element_type=F32, precision=HIGHEST_MODE)


def iota(shape, dim):
    return lax.broadcasted_iota(I32, shape, dim)


def tenth(index):
    return jnp.floor((index.astype(F32) + 0.5) * 0.1).astype(I32)


def edges_kernel(x_ref, nb_ref, head_ref, tail_ref):
    count = jnp.sum((nb_ref[0:1, :] >= 0).astype(F32), axis=1, keepdims=True)
    row = iota((2 * CAP, 2 * LANES), 0)
    lane = iota((2 * CAP, 2 * LANES), 1)
    slot = row & (CAP - 1)
    same_half = (row >= CAP) == ((lane & (LANES - 1)) >= EDGE)
    column = lane & (EDGE - 1)
    wanted = jnp.where(lane < LANES, column, column - EDGE + count.astype(I32))
    pick = ((slot == wanted) & same_half).astype(F32).astype(BF16)
    top_high, top_low = split(x_ref[0:HALF, :])
    below = jnp.concatenate([x_ref[HALF:KKK, :], jnp.zeros((2 * HALF - KKK, CAP), F32)], axis=0)
    low_high, low_low = split(below)
    both = mm(top_high, pick[:CAP]) + mm(top_low, pick[:CAP])
    both = both + (mm(low_high, pick[CAP:]) + mm(low_low, pick[CAP:]))
    head_ref[...] = both[:, :LANES]
    spot = (iota((HALF, LANES), 0) == HALF - 1) & (iota((HALF, LANES), 1) >= EDGE)
    tail_ref[...] = jnp.where(spot, count, both[:, LANES:])


def compress(value_ref, select, ff_high, ff_low, filter_smem, work_ref, out_ref):
    high, low = split(value_ref[0:KKK, :])
    span = KKK + 32
    grouped = mm_t(high, select) + mm_t(low, select)
    for w in range(4):
        work_ref[w * span : w * span + KKK, :] = grouped[:, w * LANES : (w + 1) * LANES]
        work_ref[w * span + KKK : (w + 1) * span, :] = jnp.zeros((32, LANES), F32)
    base = 4 * span
    for pair in range(5):
        columns = []
        for i in (2 * pair, 2 * pair + 1):
            columns.append(
                jnp.concatenate(
                    [work_ref[w * span + i * SQ : w * span + i * SQ + LANES, :] for w in range(4)],
                    axis=0,
                )
            )
        rhs_high, rhs_low = split(jnp.concatenate(columns, axis=1))
        z = mm(ff_high, rhs_high) + mm(ff_low, rhs_high) + mm(ff_high, rhs_low)
        work_ref[base + 208 * pair : base + 208 * pair + 104, :] = z[:, :LANES]
        work_ref[base + 208 * pair + 104 : base + 208 * pair + 208, :] = z[:, LANES:]
    upper = iota((1, LANES), 1) >= 64
    for a in range(K):
        total = None
        for i in range(K):
            weight = jnp.where(upper, filter_smem[a, 1, i], filter_smem[a, 0, i]) * CHILD_SCALE
            term = work_ref[base + 104 * i : base + 104 * i + 104, :] * weight
            total = term if total is None else total + term
        total = total + pltpu.roll(total, 64, axis=1)
        out_ref[a * SQ : (a + 1) * SQ, :] = total[:SQ]


def turned(value_ref, rows):
    high, low = split(value_ref[0:KKK, :])
    same = (iota((rows, LANES), 0) == iota((rows, LANES), 1)).astype(F32).astype(BF16)
    return mm_t(same, high) + mm_t(same, low)


def main_kernel(
    x_ref,
    left_ref,
    right_ref,
    op0_ref,
    op1_ref,
    op2_ref,
    op3_ref,
    near_ref,
    parent_one_ref,
    octant_one_ref,
    keep_ref,
    parent_two_ref,
    octant_two_ref,
    cols_ref,
    filter_ref,
    filter_smem,
    leaves_ref,
    one_ref,
    two_ref,
    send_ref,
    w_high,
    w_low,
    work,
    s_high,
    s_low,
    edge,
    b_wide,
    c_wide,
    ops,
    acc_ref,
    applied,
    level,
    level_up,
):
    ops[...] = jnp.zeros_like(ops)
    for n, ref in enumerate((op0_ref, op1_ref, op2_ref, op3_ref)):
        ops[3 * n : 3 * n + 3, 0:900] = ref[...]
    factors = ops[...]
    row = iota((104, LANES), 0)
    lane = iota((104, LANES), 1)
    spread = jnp.where(row < 80, (row >> 3) * 10 + (row & 7), 0)
    spread = jnp.where((row >= 80) & (row < 88), (row - 80) * 10 + 8, spread)
    spread = jnp.where((row >= 88) & (row < 96), (row - 88) * 10 + 9, spread)
    spread = jnp.where(row >= 96, 80 + ((row - 96) >> 1) * 10 + 8 + (row & 1), spread)
    order = ((spread == lane) & (row < 100)).astype(F32).astype(BF16)
    x_factor = []
    for code in range(3):
        moved = factors if code == 0 else pltpu.roll(factors, 1024 - SQ * code, axis=1)
        high, low = split(moved[:, :LANES])
        x_factor.append(mm_t(order, jnp.concatenate([high, low, high], axis=0)).astype(BF16))
    x_same = x_factor[0]
    x_moved = jnp.concatenate([x_factor[1], x_factor[2]], axis=0)
    column_of = iota((CAP, 512), 0)
    for wide_ref, axis in ((b_wide, 1), (c_wide, 2)):
        cols = (column_of == cols_ref[axis - 1 : axis, :]).astype(F32).astype(BF16)
        rows = [
            pltpu.roll(factors, 1024 - 300 * axis - 10 * b, axis=1)[:, :CAP] for b in range(K)
        ]
        high, low = split(jnp.concatenate(rows, axis=0))
        wide_ref[...] = (mm(high, cols) + mm(low, cols)).reshape(K, 16, 512)

    first_half = iota((HALF, LANES), 1) < EDGE
    left = left_ref[...]
    right = right_ref[...]
    edge[0:HALF, :] = jnp.where(first_half, left, pltpu.roll(right, EDGE, axis=1))
    edge[HALF : 2 * HALF, :] = jnp.where(first_half, pltpu.roll(left, EDGE, axis=1), right)
    near = near_ref[...]
    origin = near[0:1, 0:1]
    before = left[HALF - 1 : HALF, EDGE : EDGE + 1].astype(I32)
    moved = near - origin
    place = jnp.where(moved < 0, moved + (2 * CAP + EDGE) - before, moved)
    place = jnp.where(moved >= CAP, moved + EDGE, place)
    place = jnp.where(near >= 0, place, -1)
    live = (near[0:1, :] >= 0).astype(F32)
    slots = iota((CAP + LANES, CAP), 0)
    own_high, own_low = split(x_ref[...])
    far_high, far_low = split(edge[0:KKK, :])
    wide = jnp.concatenate([own_high, own_low, far_high, far_low], axis=1)
    half = KT * LANES
    for i in range(K):
        for h in range(2):
            at = h * half + i * 768
            work[at + 500 : at + 512, :] = jnp.zeros((12, LANES), F32)
            work[at + 612 : at + 640, :] = jnp.zeros((28, LANES), F32)
            work[at + 740 : at + 768, :] = jnp.zeros((28, LANES), F32)
    for e in range(7):
        if e == 0:
            taken = x_ref[...] * live
        else:
            pick = (slots == place[e : e + 1, :]).astype(F32).astype(BF16)
            taken = mm(
                wide,
                jnp.concatenate([pick[:CAP], pick[:CAP], pick[CAP:], pick[CAP:]], axis=0),
            )
        start = 0 if e == 0 else 512 if e == 1 else 640 if e == 2 else SQ * (e - 2)
        for h in range(2):
            hold = level if h == 0 else level_up
            hold[...] = taken[:, h * LANES : (h + 1) * LANES]
            for i in range(K):
                at = h * half + i * 768 + start
                work[at : at + SQ, :] = hold[i * SQ : (i + 1) * SQ, :]
    for h in range(2):
        for t in range(15):
            high, low = split(work[h * half + 512 * t : h * half + 512 * (t + 1), :])
            s_high[h, 512 * t : 512 * (t + 1), :] = high
            s_low[h, 512 * t : 512 * (t + 1), :] = low

    def build(pair_of, count, step, width):
        apart = 6 * width + 1

        def put(value, first_tile, position, tiles):
            for l in range(tiles):
                at = (first_tile + l) * width + position
                part = value[:, l * LANES : (l + 1) * LANES]
                for a in range(K):
                    work[pl.ds(at + a * step, 8, stride=apart), :] = part[8 * a : 8 * a + 8]
                for n, i in enumerate((8, 9)):
                    work[pl.ds(at + i * apart, 8, stride=step), :] = part[80 + 8 * n : 88 + 8 * n]
                for n, a in enumerate((8, 9)):
                    work[pl.ds(at + 8 * apart + a * step, 2, stride=apart), :] = part[
                        96 + 2 * n : 98 + 2 * n
                    ]

        held = []
        for u in range(count):
            b, c = pair_of(u)
            high, low = split(b_wide[b] * c_wide[c])
            rhs = jnp.concatenate([high, high, low], axis=0)
            for part in range(2):
                put(mm(x_same, rhs[:, 256 * part : 256 * part + 256]), 2 * part, u, 2)
            held.append(rhs[:, :LANES])
            if len(held) == 2:
                both = mm(x_moved, jnp.concatenate(held, axis=1))
                for n in range(2):
                    put(both[:104, n * LANES : (n + 1) * LANES], 4, u - 1 + n, 1)
                    put(both[104:, n * LANES : (n + 1) * LANES], 5, u - 1 + n, 1)
                held = []

    def one_group(g, carry):
        def pair_of(u):
            p = g * 16 + u
            b = (p * 205) >> 11
            return b, p - 10 * b

        build(pair_of, 16, 17, 170)
        first = pl.multiple_of(g * 160, 160)
        for t in range(KT):
            at = (t // 6) * 1021 + (t % 6) * 170
            for a in range(K):
                high, low = split(work[at + 17 * a : at + 17 * a + 16, :])
                w_high[t, pl.ds(first + 16 * a, 16), :] = high
                w_low[t, pl.ds(first + 16 * a, 16), :] = low
        return carry

    lax.fori_loop(0, GROUPS, one_group, 0)
    build(lambda u: (9, 6 + u), 4, 4, 48)
    for t in range(KT):
        at = (t // 6) * 289 + (t % 6) * 48
        high, low = split(work[at : at + 48, :])
        w_high[t, 960:MROWS, :] = high
        w_low[t, 960:MROWS, :] = low

    wide_high = jnp.concatenate([w_high[t] for t in range(KT)], axis=1)
    wide_low = jnp.concatenate([w_low[t] for t in range(KT)], axis=1)
    tall_high = jnp.concatenate([s_high[0], s_high[1]], axis=1)
    tall_low = jnp.concatenate([s_low[0], s_low[1]], axis=1)
    acc_ref[...] = mm(wide_high, tall_high)
    acc_ref[...] += mm(wide_low, tall_high)
    acc_ref[...] += mm(wide_high, tall_low)
    for a in range(K):
        for g in range(GROUPS):
            applied[a * SQ + 16 * g : a * SQ + 16 * g + 16, :] = acc_ref[
                g * 160 + a * 16 : g * 160 + a * 16 + 16, :
            ]
        applied[a * SQ + 96 : a * SQ + SQ, :] = acc_ref[960 + 4 * a : 964 + 4 * a, :]
    leaves_ref[...] = applied[...] * keep_ref[...].astype(F32)

    p_row = iota((104, 16), 0)
    small = iota((104, 16), 1)
    b_of = tenth(p_row)
    c_of = p_row - 10 * b_of
    pick_b = ((b_of == small) & (p_row < SQ)).astype(F32).astype(BF16)
    pick_c = ((c_of == small) & (p_row < SQ)).astype(F32).astype(BF16)
    q_lane = iota((LANES, LANES), 1)
    j_of = tenth(q_lane)
    k_of = q_lane - 10 * j_of
    small = iota((LANES, LANES), 0)
    pick_j = ((j_of == small) & (q_lane < SQ)).astype(F32).astype(BF16)
    pick_k = ((k_of == small) & (q_lane < SQ)).astype(F32).astype(BF16)
    ops[...] = jnp.zeros_like(ops)
    for f in range(2):
        ops[0:K, f * LANES : f * LANES + K] = filter_ref[:, f, :]
    high, low = split(ops[:, 0 : 2 * LANES])
    square = jnp.concatenate([high, low], axis=1)

    def spread_filter(pick_row, pick_lane):
        grown = mm(pick_row, square).astype(BF16)
        parts = [mm(grown[:, n * LANES : (n + 1) * LANES], pick_lane) for n in range(4)]
        return parts[0] + parts[2], parts[1] + parts[3]

    y_filter = spread_filter(pick_b, pick_j)
    z_filter = spread_filter(pick_c, pick_k)
    ff = jnp.concatenate(
        [y_filter[0] * z_filter[0], y_filter[1] * z_filter[0], y_filter[0] * z_filter[1], y_filter[1] * z_filter[1]],
        axis=1,
    )
    ff_high, ff_low = split(ff)
    parent = parent_one_ref[...]
    octant = octant_one_ref[...]
    local = parent - (origin >> 3)
    local = jnp.where(local < 0, 32, local)
    code = (octant >> 1) * LANES + (octant & 1) * 64 + local
    code = jnp.where(parent >= 0, code, -1)
    rows = iota((4 * LANES, CAP), 0)
    select = (rows == code).astype(F32).astype(BF16)
    compress(applied, select, ff_high, ff_low, filter_smem, work, level)
    parent = parent_two_ref[...]
    octant = octant_two_ref[...]
    local = parent - (origin >> 6)
    local = jnp.where(local < 0, 4, local)
    code = (octant >> 1) * LANES + (octant & 1) * 64 + local
    code = jnp.where(parent >= 0, code, -1)
    last = (octant[:, 0:1] + 7) & 7
    last = (last >> 1) * LANES + (last & 1) * 64 + 4
    code = jnp.concatenate([code, jnp.broadcast_to(last, (1, 32)), jnp.full((1, 64), -1, I32)], axis=1)
    rows = iota((4 * LANES, LANES), 0)
    lane = iota((4 * LANES, LANES), 1)
    select = ((rows == code) & (lane <= 32)).astype(F32).astype(BF16)
    compress(level, select, ff_high, ff_low, filter_smem, work, level_up)
    one = turned(level, 40)
    two = turned(level_up, 8)
    one_ref[...] = one[:32]
    two_ref[...] = two[:4]
    send_ref[0:1, :] = one[32:33]
    send_ref[1:2, :] = two[4:5]


def finish_kernel(one_ref, two_ref, in_ref, parent_one_ref, parent_two_ref, one_out, two_out):
    for ref, parent_ref, out, n in ((one_ref, parent_one_ref, one_out, 0), (two_ref, parent_two_ref, two_out, 1)):
        rows = ref.shape[0]
        last = jnp.max(parent_ref[...], axis=1, keepdims=True) & (rows - 1)
        mask = (iota((rows, 1), 0) == last).astype(F32)
        out[...] = ref[...] + mask * in_ref[n : n + 1, :]


def column_table():
    table = np.full((8, 512), -1, np.int32)
    for n, e in enumerate(SAME_X):
        for j in range(K):
            for k in range(K):
                at = n * SQ + j * K + k
                table[0, at] = Y_CODE[e] * SQ + j
                table[1, at] = Z_CODE[e] * SQ + k
    return table


VMEM_SPEC = pl.BlockSpec(memory_space=pltpu.VMEM)
SMEM_SPEC = pl.BlockSpec(memory_space=pltpu.SMEM)
PARAMS = pltpu.CompilerParams(vmem_limit_bytes=63 * 1024 * 1024)


def shape(dims, dtype=F32):
    return jax.ShapeDtypeStruct(dims, dtype)


def edges(coeffs, neighbours):
    return pl.pallas_call(
        edges_kernel,
        out_shape=(shape((HALF, LANES)), shape((HALF, LANES))),
        in_specs=[VMEM_SPEC] * 2,
        out_specs=(VMEM_SPEC,) * 2,
        name="edges",
    )(coeffs, neighbours)


def operator_step(coeffs, from_left, from_right, terms, ints, filters):
    turned_filters = jnp.transpose(filters, (1, 0, 2))
    return pl.pallas_call(
        main_kernel,
        out_shape=(shape((KKK, CAP)), shape((32, KKK)), shape((4, KKK)), shape((2, KKK))),
        in_specs=[VMEM_SPEC] * 15 + [SMEM_SPEC],
        out_specs=(VMEM_SPEC,) * 4,
        scratch_shapes=[
            pltpu.VMEM((KT, MROWS, LANES), BF16),
            pltpu.VMEM((KT, MROWS, LANES), BF16),
            pltpu.VMEM((2 * KT * LANES, LANES), F32),
            pltpu.VMEM((2, KT * LANES, LANES), BF16),
            pltpu.VMEM((2, KT * LANES, LANES), BF16),
            pltpu.VMEM((2 * HALF, LANES), F32),
            pltpu.VMEM((K, 16, 512), F32),
            pltpu.VMEM((K, 16, 512), F32),
            pltpu.VMEM((16, 1024), F32),
            pltpu.VMEM((MROWS, CAP), F32),
            pltpu.VMEM((KKK, CAP), F32),
            pltpu.VMEM((KKK, LANES), F32),
            pltpu.VMEM((KKK, LANES), F32),
        ],
        compiler_params=PARAMS,
        name="operator",
    )(
        coeffs,
        from_left,
        from_right,
        *terms,
        *ints,
        jnp.asarray(column_table()),
        turned_filters,
        turned_filters,
    )


def finish(one, two, received, parent_one, parent_two):
    return pl.pallas_call(
        finish_kernel,
        out_shape=(shape((32, KKK)), shape((4, KKK))),
        in_specs=[VMEM_SPEC] * 5,
        out_specs=(VMEM_SPEC,) * 2,
        name="finish",
    )(one, two, received, parent_one, parent_two)


def per_device(
    coeffs, operator, filters, neighbours, parent_one, octant_one, parent_two, octant_two, keep
):
    terms = operator.reshape(3, 900)
    others = [
        lax.ppermute(terms, "rank", [(i, (i + step) % 4) for i in range(4)]) for step in (1, 2, 3)
    ]
    head, tail = edges(coeffs, neighbours)
    count = lax.axis_size("box")
    from_left = lax.ppermute(tail, "box", [(i, i + 1) for i in range(count - 1)])
    from_right = lax.ppermute(head, "box", [(i + 1, i) for i in range(count - 1)])
    rows = [v[None] for v in (parent_one, octant_one, keep, parent_two, octant_two)]
    leaves, one, two, sent = operator_step(
        coeffs, from_left, from_right, (terms, *others), (neighbours, *rows), filters
    )
    received = lax.ppermute(sent, "box", [(i + 1, i) for i in range(count - 1)])
    one, two = finish(one, two, received, rows[0], rows[3])
    return leaves, one.T, two.T


def solution(mesh):
    placed = (
        P(None, "box"),
        P("rank", None, None, None, None),
        P(),
        P(None, "box"),
        P("box"),
        P("box"),
        P("box"),
        P("box"),
        P("box"),
    )
    return jax.shard_map(
        per_device,
        mesh=mesh,
        in_specs=placed,
        out_specs=(P(None, "box"), P(None, "box"), P(None, "box")),
        check_vma=False,
    )
```

```python
import jax
import jax.numpy as jnp
import numpy as np
from jax import lax
from jax.experimental import pallas as pl
from jax.experimental.pallas import tpu as pltpu
from jax.sharding import PartitionSpec as P

F32 = jnp.float32
BF16 = jnp.bfloat16
I32 = jnp.int32
HIGHEST_MODE = lax.Precision.HIGHEST
CHILD_SCALE = 8.0 ** (-0.5)

K = 10
SQ = 100
KKK = 1000
CAP = 256
EDGE = 64
HALF = 504
LANES = 128
KT = 60
MROWS = 1008
GROUPS = 6

SAME_X = (0, 3, 4, 5, 6)
Y_CODE = {0: 0, 3: 1, 4: 2, 5: 0, 6: 0}
Z_CODE = {0: 0, 3: 0, 4: 0, 5: 1, 6: 2}


def split(value):
    high = value.astype(BF16)
    low = (value - high.astype(F32)).astype(BF16)
    return high, low


def mm(a, b):
    return jnp.dot(a, b, preferred_element_type=F32)


def mm_t(a, b):
    return lax.dot_general(a, b, (((1,), (1,)), ((), ())), preferred_element_type=F32)


def mm_full(a, b):
    return jnp.dot(a, b, preferred_element_type=F32, precision=HIGHEST_MODE)


def iota(shape, dim):
    return lax.broadcasted_iota(I32, shape, dim)


def tenth(index):
    return jnp.floor((index.astype(F32) + 0.5) * 0.1).astype(I32)


def edges_kernel(x_ref, nb_ref, chip_ref, next_ref):
    count = jnp.sum((nb_ref[0:1, :] >= 0).astype(F32), axis=1, keepdims=True)
    row = iota((2 * CAP, 2 * LANES), 0)
    lane = iota((2 * CAP, 2 * LANES), 1)
    slot = row & (CAP - 1)
    same_half = (row >= CAP) == ((lane & (LANES - 1)) >= EDGE)
    column = lane & (EDGE - 1)
    odd = (nb_ref[0:1, 0:1] >> 8) & 1
    from_head = (lane < LANES) == (odd == 1)
    wanted = jnp.where(from_head, column, column - EDGE + count.astype(I32))
    pick = ((slot == wanted) & same_half).astype(F32).astype(BF16)
    top_high, top_low = split(x_ref[0:HALF, :])
    below = jnp.concatenate([x_ref[HALF:KKK, :], jnp.zeros((2 * HALF - KKK, CAP), F32)], axis=0)
    low_high, low_low = split(below)
    both = mm(top_high, pick[:CAP]) + mm(top_low, pick[:CAP])
    both = both + (mm(low_high, pick[CAP:]) + mm(low_low, pick[CAP:]))
    spot = (iota((HALF, LANES), 0) == HALF - 1) & (iota((HALF, LANES), 1) >= EDGE)
    chip_ref[...] = jnp.where(spot, count, both[:, :LANES])
    next_ref[...] = jnp.where(spot, count, both[:, LANES:])


def compress(value_ref, select, ff_both, filter_smem, work_ref, out_ref):
    high, low = split(value_ref[0:KKK, :])
    span = KKK + 32
    grouped = mm_t(high, select) + mm_t(low, select)
    for w in range(4):
        work_ref[w * span : w * span + KKK, :] = grouped[:, w * LANES : (w + 1) * LANES]
        work_ref[w * span + KKK : (w + 1) * span, :] = jnp.zeros((32, LANES), F32)
    base = 4 * span
    for pair in range(5):
        columns = []
        for i in (2 * pair, 2 * pair + 1):
            columns.append(
                jnp.concatenate(
                    [work_ref[w * span + i * SQ : w * span + i * SQ + LANES, :] for w in range(4)],
                    axis=0,
                )
            )
        rhs_high, rhs_low = split(jnp.concatenate(columns, axis=1))
        z = mm(ff_both, rhs_high)
        z = (z[:112] + z[112:] + mm(ff_both[:112], rhs_low))[:104]
        work_ref[base + 208 * pair : base + 208 * pair + 104, :] = z[:, :LANES]
        work_ref[base + 208 * pair + 104 : base + 208 * pair + 208, :] = z[:, LANES:]
    upper = iota((1, LANES), 1) >= 64
    for a in range(K):
        total = None
        for i in range(K):
            weight = jnp.where(upper, filter_smem[a, 1, i], filter_smem[a, 0, i]) * CHILD_SCALE
            term = work_ref[base + 104 * i : base + 104 * i + 104, :] * weight
            total = term if total is None else total + term
        total = total + pltpu.roll(total, 64, axis=1)
        out_ref[a * SQ : (a + 1) * SQ, :] = total[:SQ]


def turned(value_ref, rows):
    high, low = split(value_ref[0:KKK, :])
    same = (iota((rows, LANES), 0) == iota((rows, LANES), 1)).astype(F32).astype(BF16)
    return mm_t(same, high) + mm_t(same, low)


def main_kernel(
    x_ref,
    chip_ref,
    next_ref,
    op0_ref,
    op1_ref,
    op2_ref,
    op3_ref,
    near_ref,
    parent_one_ref,
    octant_one_ref,
    keep_ref,
    parent_two_ref,
    octant_two_ref,
    cols_ref,
    filter_ref,
    filter_smem,
    leaves_ref,
    one_ref,
    two_ref,
    send_ref,
    w_high,
    w_low,
    work,
    spare,
    s_high,
    s_low,
    edge,
    b_wide,
    c_wide,
    ops,
    level,
    level_up,
):
    ops[...] = jnp.zeros_like(ops)
    for n, ref in enumerate((op0_ref, op1_ref, op2_ref, op3_ref)):
        ops[3 * n : 3 * n + 3, 0:900] = ref[...]
    factors = ops[...]
    row = iota((104, LANES), 0)
    lane = iota((104, LANES), 1)
    spread = jnp.where(row < 80, (row >> 3) * 10 + (row & 7), 0)
    spread = jnp.where((row >= 80) & (row < 88), (row - 80) * 10 + 8, spread)
    spread = jnp.where((row >= 88) & (row < 96), (row - 88) * 10 + 9, spread)
    spread = jnp.where(row >= 96, 80 + ((row - 96) >> 1) * 10 + 8 + (row & 1), spread)
    order = ((spread == lane) & (row < 100)).astype(F32).astype(BF16)
    x_factor = []
    for code in range(3):
        moved = factors if code == 0 else pltpu.roll(factors, 1024 - SQ * code, axis=1)
        high, low = split(moved[:, :LANES])
        x_factor.append(mm_t(order, jnp.concatenate([high, low, high], axis=0)).astype(BF16))
    x_same = x_factor[0]
    x_moved = jnp.concatenate([x_factor[1], x_factor[2]], axis=0)
    column_of = iota((CAP, 512), 0)
    for wide_ref, axis in ((b_wide, 1), (c_wide, 2)):
        cols = (column_of == cols_ref[axis - 1 : axis, :]).astype(F32).astype(BF16)
        rows = [
            pltpu.roll(factors, 1024 - 300 * axis - 10 * b, axis=1)[:, :CAP] for b in range(K)
        ]
        high, low = split(jnp.concatenate(rows, axis=0))
        wide_ref[...] = (mm(high, cols) + mm(low, cols)).reshape(K, 16, 512)

    first_half = iota((HALF, LANES), 1) < EDGE
    near = near_ref[...]
    origin = near[0:1, 0:1]
    odd = ((origin >> 8) & 1) == 1
    left = jnp.where(odd, chip_ref[...], next_ref[...])
    right = jnp.where(odd, next_ref[...], chip_ref[...])
    edge[0:HALF, :] = jnp.where(first_half, left, pltpu.roll(right, EDGE, axis=1))
    edge[HALF : 2 * HALF, :] = jnp.where(first_half, pltpu.roll(left, EDGE, axis=1), right)
    before = left[HALF - 1 : HALF, EDGE : EDGE + 1].astype(I32)
    moved = near - origin
    place = jnp.where(moved < 0, moved + (2 * CAP + EDGE) - before, moved)
    place = jnp.where(moved >= CAP, moved + EDGE, place)
    place = jnp.where(near >= 0, place, -1)
    live = (near[0:1, :] >= 0).astype(F32)
    slots = iota((CAP + LANES, CAP), 0)
    own_high, own_low = split(x_ref[...])
    far_high, far_low = split(edge[0:KKK, :])
    wide = jnp.concatenate([own_high, own_low, far_high, far_low], axis=1)
    half = KT * LANES
    for i in range(K):
        for h in range(2):
            at = h * half + i * 768
            work[at + 500 : at + 512, :] = jnp.zeros((12, LANES), F32)
            work[at + 612 : at + 640, :] = jnp.zeros((28, LANES), F32)
            work[at + 740 : at + 768, :] = jnp.zeros((28, LANES), F32)
    for e in range(7):
        if e == 0:
            taken = x_ref[...] * live
        else:
            pick = (slots == place[e : e + 1, :]).astype(F32).astype(BF16)
            taken = mm(
                wide,
                jnp.concatenate([pick[:CAP], pick[:CAP], pick[CAP:], pick[CAP:]], axis=0),
            )
        start = 0 if e == 0 else 512 if e == 1 else 640 if e == 2 else SQ * (e - 2)
        for h in range(2):
            part = taken[:, h * LANES : (h + 1) * LANES]
            for i in range(K):
                at = h * half + i * 768 + start
                lead = 4 * (i % 2)
                if lead:
                    work[at : at + 4, :] = part[i * SQ - 4 : i * SQ + 4][4:]
                work[at + lead : at + SQ, :] = part[i * SQ + lead : (i + 1) * SQ]
    for h in range(2):
        for t in range(15):
            high, low = split(work[h * half + 512 * t : h * half + 512 * (t + 1), :])
            s_high[h, 512 * t : 512 * (t + 1), :] = high
            s_low[h, 512 * t : 512 * (t + 1), :] = low

    def build(stage, pair_of, count, step, width, between):
        apart = 6 * width + 1

        def put(value, first_tile, position, tiles):
            for l in range(tiles):
                at = (first_tile + l) * width + position
                part = value[:, l * LANES : (l + 1) * LANES]
                for a in range(K):
                    stage[pl.ds(at + a * step, 8, stride=apart), :] = part[8 * a : 8 * a + 8]
                for n, i in enumerate((8, 9)):
                    stage[pl.ds(at + i * apart, 8, stride=step), :] = part[80 + 8 * n : 88 + 8 * n]
                for n, a in enumerate((8, 9)):
                    stage[pl.ds(at + 8 * apart + a * step, 2, stride=apart), :] = part[
                        96 + 2 * n : 98 + 2 * n
                    ]

        held = []
        for u in range(count):
            b, c = pair_of(u)
            high, low = split(b_wide[b] * c_wide[c])
            rhs = jnp.concatenate([high, high, low], axis=0)
            for part in range(2):
                put(mm(x_same, rhs[:, 256 * part : 256 * part + 256]), 2 * part, u, 2)
            held.append(rhs[:, :LANES])
            if len(held) == 2:
                both = mm(x_moved, jnp.concatenate(held, axis=1))
                for n in range(2):
                    put(both[:104, n * LANES : (n + 1) * LANES], 4, u - 1 + n, 1)
                    put(both[104:, n * LANES : (n + 1) * LANES], 5, u - 1 + n, 1)
                held = []
            between(u)

    def pair_in(g):
        def pair_of(u):
            p = g * 16 + u
            b = (p * 205) >> 11
            return b, p - 10 * b

        return pair_of

    def convert(stage, g, count):
        first = pl.multiple_of(g * 160, 160)

        def between(u):
            for unit in range(u * KT * K // count, (u + 1) * KT * K // count):
                t, a = divmod(unit, K)
                at = (t // 6) * 1021 + (t % 6) * 170 + 17 * a
                high, low = split(stage[at : at + 16, :])
                w_high[t, pl.ds(first + 16 * a, 16), :] = high
                w_low[t, pl.ds(first + 16 * a, 16), :] = low

        return between

    def two_groups(n, carry):
        g = 2 * n
        ahead = jnp.where(n == 0, GROUPS - 1, g - 1)
        build(work, pair_in(g), 16, 17, 170, convert(spare, ahead, 16))
        build(spare, pair_in(g + 1), 16, 17, 170, convert(work, g, 16))
        return carry

    lax.fori_loop(0, GROUPS // 2, two_groups, 0)
    build(work, lambda u: (9, 6 + u), 4, 4, 48, convert(spare, GROUPS - 1, 4))
    for t in range(KT):
        at = (t // 6) * 289 + (t % 6) * 48
        high, low = split(work[at : at + 48, :])
        w_high[t, 960:MROWS, :] = high
        w_low[t, 960:MROWS, :] = low

    tall_high = jnp.concatenate([s_high[0], s_high[1]], axis=1)
    tall_low = jnp.concatenate([s_low[0], s_low[1]], axis=1)
    middle = KT // 2
    first = [w_high[t] for t in range(KT)] + [w_low[t] for t in range(middle)]
    second = [w_low[t] for t in range(middle, KT)] + [w_high[t] for t in range(KT)]
    total = mm(
        jnp.concatenate(first, axis=1),
        jnp.concatenate([tall_high, tall_high[: middle * LANES]], axis=0),
    ) + mm(
        jnp.concatenate(second, axis=1),
        jnp.concatenate([tall_high[middle * LANES :], tall_low], axis=0),
    )
    for h in range(2):
        at = h * MROWS
        columns = slice(h * LANES, (h + 1) * LANES)
        spare[at : at + MROWS, :] = total[:, columns]
        for a in range(K):
            for g in range(GROUPS):
                leaves_ref[a * SQ + 16 * g : a * SQ + 16 * g + 16, columns] = spare[
                    at + g * 160 + a * 16 : at + g * 160 + a * 16 + 16, :
                ]
            leaves_ref[a * SQ + 96 : a * SQ + SQ, columns] = spare[at + 960 + 4 * a : at + 964 + 4 * a, :]

    p_row = iota((112, 16), 0)
    small = iota((112, 16), 1)
    b_of = tenth(p_row)
    c_of = p_row - 10 * b_of
    pick_b = ((b_of == small) & (p_row < SQ)).astype(F32).astype(BF16)
    pick_c = ((c_of == small) & (p_row < SQ)).astype(F32).astype(BF16)
    q_lane = iota((LANES, LANES), 1)
    j_of = tenth(q_lane)
    k_of = q_lane - 10 * j_of
    small = iota((LANES, LANES), 0)
    pick_j = ((j_of == small) & (q_lane < SQ)).astype(F32).astype(BF16)
    pick_k = ((k_of == small) & (q_lane < SQ)).astype(F32).astype(BF16)
    ops[...] = jnp.zeros_like(ops)
    for f in range(2):
        ops[0:K, f * LANES : f * LANES + K] = filter_ref[:, f, :]
    high, low = split(ops[:, 0 : 2 * LANES])
    square = jnp.concatenate([high, low], axis=1)

    def spread_filter(pick_row, pick_lane):
        grown = mm(pick_row, square).astype(BF16)
        parts = [mm(grown[:, n * LANES : (n + 1) * LANES], pick_lane) for n in range(4)]
        return parts[0] + parts[2], parts[1] + parts[3]

    y_filter = spread_filter(pick_b, pick_j)
    z_filter = spread_filter(pick_c, pick_k)
    ff = jnp.concatenate(
        [y_filter[0] * z_filter[0], y_filter[1] * z_filter[0], y_filter[0] * z_filter[1], y_filter[1] * z_filter[1]],
        axis=1,
    )
    ff_both = jnp.concatenate(split(ff), axis=0)
    parent = parent_one_ref[...]
    octant = octant_one_ref[...]
    local = parent - (origin >> 3)
    local = jnp.where(local < 0, 32, local)
    code = (octant >> 1) * LANES + (octant & 1) * 64 + local
    code = jnp.where(parent >= 0, code, -1)
    rows = iota((4 * LANES, CAP), 0)
    select = (rows == code).astype(F32).astype(BF16)
    compress(leaves_ref, select, ff_both, filter_smem, work, level)
    leaves_ref[...] = leaves_ref[...] * keep_ref[...].astype(F32)
    parent = parent_two_ref[...]
    octant = octant_two_ref[...]
    local = parent - (origin >> 6)
    local = jnp.where(local < 0, 4, local)
    code = (octant >> 1) * LANES + (octant & 1) * 64 + local
    code = jnp.where(parent >= 0, code, -1)
    last = (octant[:, 0:1] + 7) & 7
    last = (last >> 1) * LANES + (last & 1) * 64 + 4
    code = jnp.concatenate([code, jnp.broadcast_to(last, (1, 32)), jnp.full((1, 64), -1, I32)], axis=1)
    rows = iota((4 * LANES, LANES), 0)
    lane = iota((4 * LANES, LANES), 1)
    select = ((rows == code) & (lane <= 32)).astype(F32).astype(BF16)
    compress(level, select, ff_both, filter_smem, work, level_up)
    one = turned(level, 40)
    two = turned(level_up, 8)
    one_ref[...] = one[:32]
    two_ref[...] = two[:4]
    send_ref[0:1, :] = one[32:33]
    send_ref[1:2, :] = two[4:5]


def finish_kernel(one_ref, two_ref, in_ref, parent_one_ref, parent_two_ref, one_out, two_out):
    for ref, parent_ref, out, n in ((one_ref, parent_one_ref, one_out, 0), (two_ref, parent_two_ref, two_out, 1)):
        rows = ref.shape[0]
        last = jnp.max(parent_ref[...], axis=1, keepdims=True) & (rows - 1)
        mask = (iota((rows, 1), 0) == last).astype(F32)
        out[...] = ref[...] + mask * in_ref[n : n + 1, :]


def column_table():
    table = np.full((8, 512), -1, np.int32)
    for n, e in enumerate(SAME_X):
        for j in range(K):
            for k in range(K):
                at = n * SQ + j * K + k
                table[0, at] = Y_CODE[e] * SQ + j
                table[1, at] = Z_CODE[e] * SQ + k
    return table


VMEM_SPEC = pl.BlockSpec(memory_space=pltpu.VMEM)
SMEM_SPEC = pl.BlockSpec(memory_space=pltpu.SMEM)
PARAMS = pltpu.CompilerParams(vmem_limit_bytes=63 * 1024 * 1024)


def shape(dims, dtype=F32):
    return jax.ShapeDtypeStruct(dims, dtype)


def edges(coeffs, neighbours):
    return pl.pallas_call(
        edges_kernel,
        out_shape=(shape((HALF, LANES)), shape((HALF, LANES))),
        in_specs=[VMEM_SPEC] * 2,
        out_specs=(VMEM_SPEC,) * 2,
        name="edges",
    )(coeffs, neighbours)


def operator_step(coeffs, from_left, from_right, terms, ints, filters):
    turned_filters = jnp.transpose(filters, (1, 0, 2))
    return pl.pallas_call(
        main_kernel,
        out_shape=(shape((KKK, CAP)), shape((32, KKK)), shape((4, KKK)), shape((2, KKK))),
        in_specs=[VMEM_SPEC] * 15 + [SMEM_SPEC],
        out_specs=(VMEM_SPEC,) * 4,
        scratch_shapes=[
            pltpu.VMEM((KT, MROWS, LANES), BF16),
            pltpu.VMEM((KT, MROWS, LANES), BF16),
            pltpu.VMEM((2 * KT * LANES, LANES), F32),
            pltpu.VMEM((10216, LANES), F32),
            pltpu.VMEM((2, KT * LANES, LANES), BF16),
            pltpu.VMEM((2, KT * LANES, LANES), BF16),
            pltpu.VMEM((2 * HALF, LANES), F32),
            pltpu.VMEM((K, 16, 512), F32),
            pltpu.VMEM((K, 16, 512), F32),
            pltpu.VMEM((16, 1024), F32),
            pltpu.VMEM((KKK, LANES), F32),
            pltpu.VMEM((KKK, LANES), F32),
        ],
        compiler_params=PARAMS,
        name="operator",
    )(
        coeffs,
        from_left,
        from_right,
        *terms,
        *ints,
        jnp.asarray(column_table()),
        turned_filters,
        turned_filters,
    )


def finish(one, two, received, parent_one, parent_two):
    return pl.pallas_call(
        finish_kernel,
        out_shape=(shape((32, KKK)), shape((4, KKK))),
        in_specs=[VMEM_SPEC] * 5,
        out_specs=(VMEM_SPEC,) * 2,
        name="finish",
    )(one, two, received, parent_one, parent_two)


def per_device(
    coeffs, operator, filters, neighbours, parent_one, octant_one, parent_two, octant_two, keep
):
    terms = operator.reshape(3, 900)
    others = [
        lax.ppermute(terms, "rank", [(i, i ^ step) for i in range(4)]) for step in (1, 2, 3)
    ]
    to_chip, to_next = edges(coeffs, neighbours)
    count = lax.axis_size("box")
    pairs = [(i, i ^ 1) for i in range(count)]
    across = [(i, i + 1 if i % 2 else i - 1) for i in range(1, count - 1)]
    from_chip = lax.ppermute(to_chip, "box", pairs)
    from_next = lax.ppermute(to_next, "box", across)
    rows = [v[None] for v in (parent_one, octant_one, keep, parent_two, octant_two)]
    leaves, one, two, sent = operator_step(
        coeffs, from_chip, from_next, (terms, *others), (neighbours, *rows), filters
    )
    received = lax.ppermute(sent, "box", [(i + 1, i) for i in range(count - 1)])
    one, two = finish(one, two, received, rows[0], rows[3])
    return leaves, one.T, two.T


def solution(mesh):
    placed = (
        P(None, "box"),
        P("rank", None, None, None, None),
        P(),
        P(None, "box"),
        P("box"),
        P("box"),
        P("box"),
        P("box"),
        P("box"),
    )
    return jax.shard_map(
        per_device,
        mesh=mesh,
        in_specs=placed,
        out_specs=(P(None, "box"), P(None, "box"), P(None, "box")),
        check_vma=False,
    )
```

```python
import jax
import jax.numpy as jnp
import numpy as np
from jax import lax
from jax.experimental import pallas as pl
from jax.experimental.pallas import tpu as pltpu
from jax.sharding import PartitionSpec as P

F32 = jnp.float32
BF16 = jnp.bfloat16
I32 = jnp.int32
HIGHEST_MODE = lax.Precision.HIGHEST
CHILD_SCALE = 8.0 ** (-0.5)

K = 10
SQ = 100
KKK = 1000
CAP = 256
EDGE = 64
HALF = 504
LANES = 128
KT = 60
A_STEP = 101
TILE = 1016
I_STEP = 6 * TILE + 1
DENSE_ROWS = 60984

SAME_X = (0, 3, 4, 5, 6)
Y_CODE = {0: 0, 3: 1, 4: 2, 5: 0, 6: 0}
Z_CODE = {0: 0, 3: 0, 4: 0, 5: 1, 6: 2}


def split(value):
    high = value.astype(BF16)
    low = (value - high.astype(F32)).astype(BF16)
    return high, low


def mm(a, b):
    return jnp.dot(a, b, preferred_element_type=F32)


def mm_t(a, b):
    return lax.dot_general(a, b, (((1,), (1,)), ((), ())), preferred_element_type=F32)


def mm_full(a, b):
    return jnp.dot(a, b, preferred_element_type=F32, precision=HIGHEST_MODE)


def iota(shape, dim):
    return lax.broadcasted_iota(I32, shape, dim)


def tenth(index):
    return jnp.floor((index.astype(F32) + 0.5) * 0.1).astype(I32)


def edges_kernel(x_ref, nb_ref, chip_ref, next_ref):
    count = jnp.sum((nb_ref[0:1, :] >= 0).astype(F32), axis=1, keepdims=True)
    row = iota((2 * CAP, 2 * LANES), 0)
    lane = iota((2 * CAP, 2 * LANES), 1)
    slot = row & (CAP - 1)
    same_half = (row >= CAP) == ((lane & (LANES - 1)) >= EDGE)
    column = lane & (EDGE - 1)
    odd = (nb_ref[0:1, 0:1] >> 8) & 1
    from_head = (lane < LANES) == (odd == 1)
    wanted = jnp.where(from_head, column, column - EDGE + count.astype(I32))
    pick = ((slot == wanted) & same_half).astype(F32).astype(BF16)
    top_high, top_low = split(x_ref[0:HALF, :])
    below = jnp.concatenate([x_ref[HALF:KKK, :], jnp.zeros((2 * HALF - KKK, CAP), F32)], axis=0)
    low_high, low_low = split(below)
    both = mm(top_high, pick[:CAP]) + mm(top_low, pick[:CAP])
    both = both + (mm(low_high, pick[CAP:]) + mm(low_low, pick[CAP:]))
    spot = (iota((HALF, LANES), 0) == HALF - 1) & (iota((HALF, LANES), 1) >= EDGE)
    chip_ref[...] = jnp.where(spot, count, both[:, :LANES])
    next_ref[...] = jnp.where(spot, count, both[:, LANES:])


def compress(value_ref, select, ff_both, filter_smem, work_ref, out_ref):
    high, low = split(value_ref[0:KKK, :])
    span = KKK + 32
    grouped = mm_t(high, select) + mm_t(low, select)
    for w in range(4):
        work_ref[w * span : w * span + KKK, :] = grouped[:, w * LANES : (w + 1) * LANES]
        work_ref[w * span + KKK : (w + 1) * span, :] = jnp.zeros((32, LANES), F32)
    base = 4 * span
    for pair in range(5):
        columns = []
        for i in (2 * pair, 2 * pair + 1):
            columns.append(
                jnp.concatenate(
                    [work_ref[w * span + i * SQ : w * span + i * SQ + LANES, :] for w in range(4)],
                    axis=0,
                )
            )
        rhs_high, rhs_low = split(jnp.concatenate(columns, axis=1))
        z = mm(ff_both, rhs_high)
        z = (z[:112] + z[112:] + mm(ff_both[:112], rhs_low))[:104]
        work_ref[base + 208 * pair : base + 208 * pair + 104, :] = z[:, :LANES]
        work_ref[base + 208 * pair + 104 : base + 208 * pair + 208, :] = z[:, LANES:]
    upper = iota((1, LANES), 1) >= 64
    for a in range(K):
        total = None
        for i in range(K):
            weight = jnp.where(upper, filter_smem[a, 1, i], filter_smem[a, 0, i]) * CHILD_SCALE
            term = work_ref[base + 104 * i : base + 104 * i + 104, :] * weight
            total = term if total is None else total + term
        total = total + pltpu.roll(total, 64, axis=1)
        out_ref[a * SQ : (a + 1) * SQ, :] = total[:SQ]


def turned(value_ref, rows):
    high, low = split(value_ref[0:KKK, :])
    same = (iota((rows, LANES), 0) == iota((rows, LANES), 1)).astype(F32).astype(BF16)
    return mm_t(same, high) + mm_t(same, low)


def main_kernel(
    x_ref,
    chip_ref,
    next_ref,
    op0_ref,
    op1_ref,
    op2_ref,
    op3_ref,
    near_ref,
    parent_one_ref,
    octant_one_ref,
    keep_ref,
    parent_two_ref,
    octant_two_ref,
    cols_ref,
    filter_ref,
    filter_smem,
    leaves_ref,
    one_ref,
    two_ref,
    send_ref,
    dense,
    work,
    s_high,
    s_low,
    edge,
    b_wide,
    c_wide,
    ops,
    level,
    level_up,
):
    ops[...] = jnp.zeros_like(ops)
    for n, ref in enumerate((op0_ref, op1_ref, op2_ref, op3_ref)):
        ops[3 * n : 3 * n + 3, 0:900] = ref[...]
    factors = ops[...]
    row = iota((104, LANES), 0)
    lane = iota((104, LANES), 1)
    spread = jnp.where(row < 80, (row >> 3) * 10 + (row & 7), 0)
    spread = jnp.where((row >= 80) & (row < 88), (row - 80) * 10 + 8, spread)
    spread = jnp.where((row >= 88) & (row < 96), (row - 88) * 10 + 9, spread)
    spread = jnp.where(row >= 96, 80 + ((row - 96) >> 1) * 10 + 8 + (row & 1), spread)
    order = ((spread == lane) & (row < 100)).astype(F32).astype(BF16)
    x_factor = []
    for code in range(3):
        moved = factors if code == 0 else pltpu.roll(factors, 1024 - SQ * code, axis=1)
        high, low = split(moved[:, :LANES])
        x_factor.append(mm_t(order, jnp.concatenate([high, low, high], axis=0)).astype(BF16))
    x_same = x_factor[0]
    x_moved = jnp.concatenate([x_factor[1], x_factor[2]], axis=0)
    column_of = iota((CAP, 512), 0)
    for wide_ref, axis in ((b_wide, 1), (c_wide, 2)):
        cols = (column_of == cols_ref[axis - 1 : axis, :]).astype(F32).astype(BF16)
        rows = [
            pltpu.roll(factors, 1024 - 300 * axis - 10 * b, axis=1)[:, :CAP] for b in range(K)
        ]
        high, low = split(jnp.concatenate(rows, axis=0))
        wide_ref[...] = (mm(high, cols) + mm(low, cols)).reshape(K, 16, 512)

    first_half = iota((HALF, LANES), 1) < EDGE
    near = near_ref[...]
    origin = near[0:1, 0:1]
    odd = ((origin >> 8) & 1) == 1
    left = jnp.where(odd, chip_ref[...], next_ref[...])
    right = jnp.where(odd, next_ref[...], chip_ref[...])
    edge[0:HALF, :] = jnp.where(first_half, left, pltpu.roll(right, EDGE, axis=1))
    edge[HALF : 2 * HALF, :] = jnp.where(first_half, pltpu.roll(left, EDGE, axis=1), right)
    before = left[HALF - 1 : HALF, EDGE : EDGE + 1].astype(I32)
    moved = near - origin
    place = jnp.where(moved < 0, moved + (2 * CAP + EDGE) - before, moved)
    place = jnp.where(moved >= CAP, moved + EDGE, place)
    place = jnp.where(near >= 0, place, -1)
    live = (near[0:1, :] >= 0).astype(F32)
    slots = iota((CAP + LANES, CAP), 0)
    own_high, own_low = split(x_ref[...])
    far_high, far_low = split(edge[0:KKK, :])
    wide = jnp.concatenate([own_high, own_low, far_high, far_low], axis=1)
    half = KT * LANES
    for i in range(K):
        for h in range(2):
            at = h * half + i * 768
            work[at + 500 : at + 512, :] = jnp.zeros((12, LANES), F32)
            work[at + 612 : at + 640, :] = jnp.zeros((28, LANES), F32)
            work[at + 740 : at + 768, :] = jnp.zeros((28, LANES), F32)
    for e in range(7):
        if e == 0:
            taken = x_ref[...] * live
        else:
            pick = (slots == place[e : e + 1, :]).astype(F32).astype(BF16)
            taken = mm(
                wide,
                jnp.concatenate([pick[:CAP], pick[:CAP], pick[CAP:], pick[CAP:]], axis=0),
            )
        start = 0 if e == 0 else 512 if e == 1 else 640 if e == 2 else SQ * (e - 2)
        for h in range(2):
            part = taken[:, h * LANES : (h + 1) * LANES]
            for i in range(K):
                at = h * half + i * 768 + start
                lead = 4 * (i % 2)
                if lead:
                    work[at : at + 4, :] = part[i * SQ - 4 : i * SQ + 4][4:]
                work[at + lead : at + SQ, :] = part[i * SQ + lead : (i + 1) * SQ]
    for h in range(2):
        for t in range(15):
            high, low = split(work[h * half + 512 * t : h * half + 512 * (t + 1), :])
            s_high[h, 512 * t : 512 * (t + 1), :] = high
            s_low[h, 512 * t : 512 * (t + 1), :] = low

    def put(value, l, p):
        at = l * TILE + p
        for a in range(K):
            dense[pl.ds(at + a * A_STEP, 8, stride=I_STEP), :] = value[8 * a : 8 * a + 8]
        for n, i in enumerate((8, 9)):
            dense[pl.ds(at + i * I_STEP, 8, stride=A_STEP), :] = value[80 + 8 * n : 88 + 8 * n]
        for n, a in enumerate((8, 9)):
            dense[pl.ds(at + 8 * I_STEP + a * A_STEP, 2, stride=I_STEP), :] = value[
                96 + 2 * n : 98 + 2 * n
            ]

    def one_b(b, carry):
        y_part = b_wide[b]
        held = []
        for c in range(K):
            p = b * K + c
            high, low = split(y_part * c_wide[c])
            rhs = jnp.concatenate([high, high, low], axis=0)
            for part in range(2):
                both = mm(x_same, rhs[:, 256 * part : 256 * part + 256])
                for n in range(2):
                    put(both[:, n * LANES : (n + 1) * LANES], 2 * part + n, p)
            held.append(rhs[:, :LANES])
            if len(held) == 2:
                both = mm(x_moved, jnp.concatenate(held, axis=1))
                for n in range(2):
                    put(both[:104, n * LANES : (n + 1) * LANES], 4, p - 1 + n)
                    put(both[104:, n * LANES : (n + 1) * LANES], 5, p - 1 + n)
                held = []
        return carry

    lax.fori_loop(0, K, one_b, 0)

    for pair in range(5):
        at = 2 * pair * 768
        tall_high = jnp.concatenate([s_high[h, at : at + 1536, :] for h in range(2)], axis=1)
        tall_low = jnp.concatenate([s_low[h, at : at + 1536, :] for h in range(2)], axis=1)
        tall = jnp.concatenate([tall_high, tall_high, tall_low], axis=0)
        for m in range(2):
            highs = []
            lows = []
            for i in (2 * pair, 2 * pair + 1):
                for l in range(6):
                    first = i * I_STEP + l * TILE + 512 * m
                    high, low = split(dense[first : first + 512, :])
                    highs.append(high)
                    lows.append(low)
            total = mm(jnp.concatenate(highs + lows + highs, axis=1), tall)
            for h in range(2):
                rows = slice(h * 1024 + 512 * m, h * 1024 + 512 * m + 512)
                part = total[:, h * LANES : (h + 1) * LANES]
                if pair == 0:
                    work[rows, :] = part
                else:
                    work[rows, :] += part
    for h in range(2):
        for a in range(K):
            first = h * 1024 + a * A_STEP
            leaves_ref[a * SQ : (a + 1) * SQ, h * LANES : (h + 1) * LANES] = work[first : first + SQ, :]

    p_row = iota((112, 16), 0)
    small = iota((112, 16), 1)
    b_of = tenth(p_row)
    c_of = p_row - 10 * b_of
    pick_b = ((b_of == small) & (p_row < SQ)).astype(F32).astype(BF16)
    pick_c = ((c_of == small) & (p_row < SQ)).astype(F32).astype(BF16)
    q_lane = iota((LANES, LANES), 1)
    j_of = tenth(q_lane)
    k_of = q_lane - 10 * j_of
    small = iota((LANES, LANES), 0)
    pick_j = ((j_of == small) & (q_lane < SQ)).astype(F32).astype(BF16)
    pick_k = ((k_of == small) & (q_lane < SQ)).astype(F32).astype(BF16)
    ops[...] = jnp.zeros_like(ops)
    for f in range(2):
        ops[0:K, f * LANES : f * LANES + K] = filter_ref[:, f, :]
    high, low = split(ops[:, 0 : 2 * LANES])
    square = jnp.concatenate([high, low], axis=1)

    def spread_filter(pick_row, pick_lane):
        grown = mm(pick_row, square).astype(BF16)
        parts = [mm(grown[:, n * LANES : (n + 1) * LANES], pick_lane) for n in range(4)]
        return parts[0] + parts[2], parts[1] + parts[3]

    y_filter = spread_filter(pick_b, pick_j)
    z_filter = spread_filter(pick_c, pick_k)
    ff = jnp.concatenate(
        [y_filter[0] * z_filter[0], y_filter[1] * z_filter[0], y_filter[0] * z_filter[1], y_filter[1] * z_filter[1]],
        axis=1,
    )
    ff_both = jnp.concatenate(split(ff), axis=0)
    parent = parent_one_ref[...]
    octant = octant_one_ref[...]
    local = parent - (origin >> 3)
    local = jnp.where(local < 0, 32, local)
    code = (octant >> 1) * LANES + (octant & 1) * 64 + local
    code = jnp.where(parent >= 0, code, -1)
    rows = iota((4 * LANES, CAP), 0)
    select = (rows == code).astype(F32).astype(BF16)
    compress(leaves_ref, select, ff_both, filter_smem, work, level)
    leaves_ref[...] = leaves_ref[...] * keep_ref[...].astype(F32)
    parent = parent_two_ref[...]
    octant = octant_two_ref[...]
    local = parent - (origin >> 6)
    local = jnp.where(local < 0, 4, local)
    code = (octant >> 1) * LANES + (octant & 1) * 64 + local
    code = jnp.where(parent >= 0, code, -1)
    last = (octant[:, 0:1] + 7) & 7
    last = (last >> 1) * LANES + (last & 1) * 64 + 4
    code = jnp.concatenate([code, jnp.broadcast_to(last, (1, 32)), jnp.full((1, 64), -1, I32)], axis=1)
    rows = iota((4 * LANES, LANES), 0)
    lane = iota((4 * LANES, LANES), 1)
    select = ((rows == code) & (lane <= 32)).astype(F32).astype(BF16)
    compress(level, select, ff_both, filter_smem, work, level_up)
    one = turned(level, 40)
    two = turned(level_up, 8)
    one_ref[...] = one[:32]
    two_ref[...] = two[:4]
    send_ref[0:1, :] = one[32:33]
    send_ref[1:2, :] = two[4:5]


def finish_kernel(one_ref, two_ref, in_ref, parent_one_ref, parent_two_ref, one_out, two_out):
    for ref, parent_ref, out, n in ((one_ref, parent_one_ref, one_out, 0), (two_ref, parent_two_ref, two_out, 1)):
        rows = ref.shape[0]
        last = jnp.max(parent_ref[...], axis=1, keepdims=True) & (rows - 1)
        mask = (iota((rows, 1), 0) == last).astype(F32)
        out[...] = ref[...] + mask * in_ref[n : n + 1, :]


def column_table():
    table = np.full((8, 512), -1, np.int32)
    for n, e in enumerate(SAME_X):
        for j in range(K):
            for k in range(K):
                at = n * SQ + j * K + k
                table[0, at] = Y_CODE[e] * SQ + j
                table[1, at] = Z_CODE[e] * SQ + k
    return table


VMEM_SPEC = pl.BlockSpec(memory_space=pltpu.VMEM)
SMEM_SPEC = pl.BlockSpec(memory_space=pltpu.SMEM)
PARAMS = pltpu.CompilerParams(vmem_limit_bytes=63 * 1024 * 1024)


def shape(dims, dtype=F32):
    return jax.ShapeDtypeStruct(dims, dtype)


def edges(coeffs, neighbours):
    return pl.pallas_call(
        edges_kernel,
        out_shape=(shape((HALF, LANES)), shape((HALF, LANES))),
        in_specs=[VMEM_SPEC] * 2,
        out_specs=(VMEM_SPEC,) * 2,
        name="edges",
    )(coeffs, neighbours)


def operator_step(coeffs, from_left, from_right, terms, ints, filters):
    turned_filters = jnp.transpose(filters, (1, 0, 2))
    return pl.pallas_call(
        main_kernel,
        out_shape=(shape((KKK, CAP)), shape((32, KKK)), shape((4, KKK)), shape((2, KKK))),
        in_specs=[VMEM_SPEC] * 15 + [SMEM_SPEC],
        out_specs=(VMEM_SPEC,) * 4,
        scratch_shapes=[
            pltpu.VMEM((DENSE_ROWS, LANES), F32),
            pltpu.VMEM((2 * KT * LANES, LANES), F32),
            pltpu.VMEM((2, KT * LANES, LANES), BF16),
            pltpu.VMEM((2, KT * LANES, LANES), BF16),
            pltpu.VMEM((2 * HALF, LANES), F32),
            pltpu.VMEM((K, 16, 512), F32),
            pltpu.VMEM((K, 16, 512), F32),
            pltpu.VMEM((16, 1024), F32),
            pltpu.VMEM((KKK, LANES), F32),
            pltpu.VMEM((KKK, LANES), F32),
        ],
        compiler_params=PARAMS,
        name="operator",
    )(
        coeffs,
        from_left,
        from_right,
        *terms,
        *ints,
        jnp.asarray(column_table()),
        turned_filters,
        turned_filters,
    )


def finish(one, two, received, parent_one, parent_two):
    return pl.pallas_call(
        finish_kernel,
        out_shape=(shape((32, KKK)), shape((4, KKK))),
        in_specs=[VMEM_SPEC] * 5,
        out_specs=(VMEM_SPEC,) * 2,
        name="finish",
    )(one, two, received, parent_one, parent_two)


def per_device(
    coeffs, operator, filters, neighbours, parent_one, octant_one, parent_two, octant_two, keep
):
    terms = operator.reshape(3, 900)
    others = [
        lax.ppermute(terms, "rank", [(i, i ^ step) for i in range(4)]) for step in (1, 2, 3)
    ]
    to_chip, to_next = edges(coeffs, neighbours)
    count = lax.axis_size("box")
    pairs = [(i, i ^ 1) for i in range(count)]
    across = [(i, i + 1 if i % 2 else i - 1) for i in range(1, count - 1)]
    from_chip = lax.ppermute(to_chip, "box", pairs)
    from_next = lax.ppermute(to_next, "box", across)
    rows = [v[None] for v in (parent_one, octant_one, keep, parent_two, octant_two)]
    leaves, one, two, sent = operator_step(
        coeffs, from_chip, from_next, (terms, *others), (neighbours, *rows), filters
    )
    received = lax.ppermute(sent, "box", [(i + 1, i) for i in range(count - 1)])
    one, two = finish(one, two, received, rows[0], rows[3])
    return leaves, one.T, two.T


def solution(mesh):
    placed = (
        P(None, "box"),
        P("rank", None, None, None, None),
        P(),
        P(None, "box"),
        P("box"),
        P("box"),
        P("box"),
        P("box"),
        P("box"),
    )
    return jax.shard_map(
        per_device,
        mesh=mesh,
        in_specs=placed,
        out_specs=(P(None, "box"), P(None, "box"), P(None, "box")),
        check_vma=False,
    )
```

```python
import jax
import jax.numpy as jnp
import numpy as np
from jax import lax
from jax.experimental import pallas as pl
from jax.experimental.pallas import tpu as pltpu
from jax.sharding import PartitionSpec as P

F32 = jnp.float32
BF16 = jnp.bfloat16
I32 = jnp.int32
HIGHEST_MODE = lax.Precision.HIGHEST
CHILD_SCALE = 8.0 ** (-0.5)

K = 10
SQ = 100
KKK = 1000
CAP = 256
EDGE = 64
HALF = 504
LANES = 128
KT = 60
A_STEP = 101
TILE = 1016
I_STEP = 6 * TILE + 1
DENSE_ROWS = 60984

SAME_X = (0, 3, 4, 5, 6)
Y_CODE = {0: 0, 3: 1, 4: 2, 5: 0, 6: 0}
Z_CODE = {0: 0, 3: 0, 4: 0, 5: 1, 6: 2}


def split(value):
    high = value.astype(BF16)
    low = (value - high.astype(F32)).astype(BF16)
    return high, low


def mm(a, b):
    return jnp.dot(a, b, preferred_element_type=F32)


def mm_t(a, b):
    return lax.dot_general(a, b, (((1,), (1,)), ((), ())), preferred_element_type=F32)


def mm_full(a, b):
    return jnp.dot(a, b, preferred_element_type=F32, precision=HIGHEST_MODE)


def iota(shape, dim):
    return lax.broadcasted_iota(I32, shape, dim)


def place_of(a):
    return a * A_STEP - max(a - 7, 0)


def tenth(index):
    return jnp.floor((index.astype(F32) + 0.5) * 0.1).astype(I32)


def edges_kernel(x_ref, nb_ref, chip_ref, next_ref):
    count = jnp.sum((nb_ref[0:1, :] >= 0).astype(F32), axis=1, keepdims=True)
    row = iota((2 * CAP, 2 * LANES), 0)
    lane = iota((2 * CAP, 2 * LANES), 1)
    slot = row & (CAP - 1)
    same_half = (row >= CAP) == ((lane & (LANES - 1)) >= EDGE)
    column = lane & (EDGE - 1)
    odd = (nb_ref[0:1, 0:1] >> 8) & 1
    from_head = (lane < LANES) == (odd == 1)
    wanted = jnp.where(from_head, column, column - EDGE + count.astype(I32))
    pick = ((slot == wanted) & same_half).astype(F32).astype(BF16)
    top_high, top_low = split(x_ref[0:HALF, :])
    below = jnp.concatenate([x_ref[HALF:KKK, :], jnp.zeros((2 * HALF - KKK, CAP), F32)], axis=0)
    low_high, low_low = split(below)
    both = mm(top_high, pick[:CAP]) + mm(top_low, pick[:CAP])
    both = both + (mm(low_high, pick[CAP:]) + mm(low_low, pick[CAP:]))
    spot = (iota((HALF, LANES), 0) == HALF - 1) & (iota((HALF, LANES), 1) >= EDGE)
    chip_ref[...] = jnp.where(spot, count, both[:, :LANES])
    next_ref[...] = jnp.where(spot, count, both[:, LANES:])


def compress(value_ref, select, ff_both, filter_smem, work_ref, out_ref):
    high, low = split(value_ref[0:KKK, :])
    span = KKK + 32
    grouped = mm_t(high, select) + mm_t(low, select)
    for w in range(4):
        work_ref[w * span : w * span + KKK, :] = grouped[:, w * LANES : (w + 1) * LANES]
        work_ref[w * span + KKK : (w + 1) * span, :] = jnp.zeros((32, LANES), F32)
    base = 4 * span
    for pair in range(5):
        columns = []
        for i in (2 * pair, 2 * pair + 1):
            columns.append(
                jnp.concatenate(
                    [work_ref[w * span + i * SQ : w * span + i * SQ + LANES, :] for w in range(4)],
                    axis=0,
                )
            )
        rhs_high, rhs_low = split(jnp.concatenate(columns, axis=1))
        z = mm(ff_both, rhs_high)
        z = (z[:112] + z[112:] + mm(ff_both[:112], rhs_low))[:104]
        work_ref[base + 208 * pair : base + 208 * pair + 104, :] = z[:, :LANES]
        work_ref[base + 208 * pair + 104 : base + 208 * pair + 208, :] = z[:, LANES:]
    upper = iota((1, LANES), 1) >= 64
    for a in range(K):
        total = None
        for i in range(K):
            weight = jnp.where(upper, filter_smem[a, 1, i], filter_smem[a, 0, i]) * CHILD_SCALE
            term = work_ref[base + 104 * i : base + 104 * i + 104, :] * weight
            total = term if total is None else total + term
        total = total + pltpu.roll(total, 64, axis=1)
        out_ref[a * SQ : (a + 1) * SQ, :] = total[:SQ]


def turned(value_ref, rows):
    high, low = split(value_ref[0:KKK, :])
    same = (iota((rows, LANES), 0) == iota((rows, LANES), 1)).astype(F32).astype(BF16)
    return mm_t(same, high) + mm_t(same, low)


def main_kernel(
    x_ref,
    chip_ref,
    next_ref,
    op0_ref,
    op1_ref,
    op2_ref,
    op3_ref,
    near_ref,
    parent_one_ref,
    octant_one_ref,
    keep_ref,
    parent_two_ref,
    octant_two_ref,
    cols_ref,
    filter_ref,
    filter_smem,
    leaves_ref,
    one_ref,
    two_ref,
    send_ref,
    dense,
    work,
    s_high,
    s_low,
    edge,
    b_wide,
    c_wide,
    ops,
    level,
    level_up,
):
    ops[...] = jnp.zeros_like(ops)
    for n, ref in enumerate((op0_ref, op1_ref, op2_ref, op3_ref)):
        ops[3 * n : 3 * n + 3, 0:900] = ref[...]
    factors = ops[...]
    row = iota((104, LANES), 0)
    lane = iota((104, LANES), 1)
    spread = jnp.where(row < 80, (row >> 3) * 10 + (row & 7), 0)
    spread = jnp.where((row >= 80) & (row < 88), (row - 80) * 10 + 8, spread)
    spread = jnp.where((row >= 88) & (row < 96), (row - 88) * 10 + 9, spread)
    spread = jnp.where(row >= 96, 80 + ((row - 96) >> 1) * 10 + 8 + (row & 1), spread)
    order = ((spread == lane) & (row < 100)).astype(F32).astype(BF16)
    x_factor = []
    for code in range(3):
        moved = factors if code == 0 else pltpu.roll(factors, 1024 - SQ * code, axis=1)
        high, low = split(moved[:, :LANES])
        x_factor.append(mm_t(order, jnp.concatenate([high, low, high], axis=0)).astype(BF16))
    x_same = x_factor[0]
    x_moved = jnp.concatenate([x_factor[1], x_factor[2]], axis=0)
    column_of = iota((CAP, 512), 0)
    for wide_ref, axis in ((b_wide, 1), (c_wide, 2)):
        cols = (column_of == cols_ref[axis - 1 : axis, :]).astype(F32).astype(BF16)
        rows = [
            pltpu.roll(factors, 1024 - 300 * axis - 10 * b, axis=1)[:, :CAP] for b in range(K)
        ]
        high, low = split(jnp.concatenate(rows, axis=0))
        wide_ref[...] = (mm(high, cols) + mm(low, cols)).reshape(K, 16, 512)

    first_half = iota((HALF, LANES), 1) < EDGE
    near = near_ref[...]
    origin = near[0:1, 0:1]
    odd = ((origin >> 8) & 1) == 1
    left = jnp.where(odd, chip_ref[...], next_ref[...])
    right = jnp.where(odd, next_ref[...], chip_ref[...])
    edge[0:HALF, :] = jnp.where(first_half, left, pltpu.roll(right, EDGE, axis=1))
    edge[HALF : 2 * HALF, :] = jnp.where(first_half, pltpu.roll(left, EDGE, axis=1), right)
    before = left[HALF - 1 : HALF, EDGE : EDGE + 1].astype(I32)
    moved = near - origin
    place = jnp.where(moved < 0, moved + (2 * CAP + EDGE) - before, moved)
    place = jnp.where(moved >= CAP, moved + EDGE, place)
    place = jnp.where(near >= 0, place, -1)
    live = (near[0:1, :] >= 0).astype(F32)
    slots = iota((CAP + LANES, CAP), 0)
    own_high, own_low = split(x_ref[...])
    far_high, far_low = split(edge[0:KKK, :])
    wide = jnp.concatenate([own_high, own_low, far_high, far_low], axis=1)
    half = KT * LANES
    for i in range(K):
        for h in range(2):
            at = h * half + i * 768
            work[at + 500 : at + 512, :] = jnp.zeros((12, LANES), F32)
            work[at + 612 : at + 640, :] = jnp.zeros((28, LANES), F32)
            work[at + 740 : at + 768, :] = jnp.zeros((28, LANES), F32)
    for e in range(7):
        if e == 0:
            taken = x_ref[...] * live
        else:
            pick = (slots == place[e : e + 1, :]).astype(F32).astype(BF16)
            taken = mm(
                wide,
                jnp.concatenate([pick[:CAP], pick[:CAP], pick[CAP:], pick[CAP:]], axis=0),
            )
        start = 0 if e == 0 else 512 if e == 1 else 640 if e == 2 else SQ * (e - 2)
        for h in range(2):
            part = taken[:, h * LANES : (h + 1) * LANES]
            for i in range(K):
                at = h * half + i * 768 + start
                lead = 4 * (i % 2)
                if lead:
                    work[at : at + 4, :] = part[i * SQ - 4 : i * SQ + 4][4:]
                work[at + lead : at + SQ, :] = part[i * SQ + lead : (i + 1) * SQ]
    for h in range(2):
        for t in range(15):
            high, low = split(work[h * half + 512 * t : h * half + 512 * (t + 1), :])
            s_high[h, 512 * t : 512 * (t + 1), :] = high
            s_low[h, 512 * t : 512 * (t + 1), :] = low

    def put(value, l, p):
        at = l * TILE + p
        for a in range(K):
            dense[pl.ds(at + place_of(a), 8, stride=I_STEP), :] = value[8 * a : 8 * a + 8]
        for n, i in enumerate((8, 9)):
            dense[pl.ds(at + i * I_STEP, 8, stride=A_STEP), :] = value[80 + 8 * n : 88 + 8 * n]
        for n, a in enumerate((8, 9)):
            dense[pl.ds(at + 8 * I_STEP + place_of(a), 2, stride=I_STEP), :] = value[
                96 + 2 * n : 98 + 2 * n
            ]

    def one_b(b, carry):
        y_part = b_wide[b]
        held = []
        for c in range(K):
            p = b * K + c
            high, low = split(y_part * c_wide[c])
            rhs = jnp.concatenate([high, high, low], axis=0)
            for part in range(2):
                both = mm(x_same, rhs[:, 256 * part : 256 * part + 256])
                for n in range(2):
                    put(both[:, n * LANES : (n + 1) * LANES], 2 * part + n, p)
            held.append(rhs[:, :LANES])
            if len(held) == 2:
                both = mm(x_moved, jnp.concatenate(held, axis=1))
                for n in range(2):
                    put(both[:104, n * LANES : (n + 1) * LANES], 4, p - 1 + n)
                    put(both[104:, n * LANES : (n + 1) * LANES], 5, p - 1 + n)
                held = []
        return carry

    lax.fori_loop(0, K, one_b, 0)

    for pair in range(5):
        at = 2 * pair * 768
        tall_high = jnp.concatenate([s_high[h, at : at + 1536, :] for h in range(2)], axis=1)
        tall_low = jnp.concatenate([s_low[h, at : at + 1536, :] for h in range(2)], axis=1)
        tall = jnp.concatenate([tall_high, tall_high, tall_low], axis=0)
        for m in range(2):
            highs = []
            lows = []
            for i in (2 * pair, 2 * pair + 1):
                for l in range(6):
                    first = i * I_STEP + l * TILE + 512 * m
                    high, low = split(dense[first : first + 512 - 16 * m, :])
                    highs.append(high)
                    lows.append(low)
            total = mm(jnp.concatenate(highs + lows + highs, axis=1), tall)
            for h in range(2):
                rows = slice(h * 1024 + 512 * m, h * 1024 + 1024 * m + 512 * (1 - m) - 16 * m)
                part = total[:, h * LANES : (h + 1) * LANES]
                if pair == 0:
                    work[rows, :] = part
                else:
                    work[rows, :] += part
    for h in range(2):
        for a in range(K):
            first = h * 1024 + place_of(a)
            leaves_ref[a * SQ : (a + 1) * SQ, h * LANES : (h + 1) * LANES] = work[first : first + SQ, :]

    p_row = iota((112, 16), 0)
    small = iota((112, 16), 1)
    b_of = tenth(p_row)
    c_of = p_row - 10 * b_of
    pick_b = ((b_of == small) & (p_row < SQ)).astype(F32).astype(BF16)
    pick_c = ((c_of == small) & (p_row < SQ)).astype(F32).astype(BF16)
    q_lane = iota((LANES, LANES), 1)
    j_of = tenth(q_lane)
    k_of = q_lane - 10 * j_of
    small = iota((LANES, LANES), 0)
    pick_j = ((j_of == small) & (q_lane < SQ)).astype(F32).astype(BF16)
    pick_k = ((k_of == small) & (q_lane < SQ)).astype(F32).astype(BF16)
    ops[...] = jnp.zeros_like(ops)
    for f in range(2):
        ops[0:K, f * LANES : f * LANES + K] = filter_ref[:, f, :]
    high, low = split(ops[:, 0 : 2 * LANES])
    square = jnp.concatenate([high, low], axis=1)

    def spread_filter(pick_row, pick_lane):
        grown = mm(pick_row, square).astype(BF16)
        parts = [mm(grown[:, n * LANES : (n + 1) * LANES], pick_lane) for n in range(4)]
        return parts[0] + parts[2], parts[1] + parts[3]

    y_filter = spread_filter(pick_b, pick_j)
    z_filter = spread_filter(pick_c, pick_k)
    ff = jnp.concatenate(
        [y_filter[0] * z_filter[0], y_filter[1] * z_filter[0], y_filter[0] * z_filter[1], y_filter[1] * z_filter[1]],
        axis=1,
    )
    ff_both = jnp.concatenate(split(ff), axis=0)
    parent = parent_one_ref[...]
    octant = octant_one_ref[...]
    local = parent - (origin >> 3)
    local = jnp.where(local < 0, 32, local)
    code = (octant >> 1) * LANES + (octant & 1) * 64 + local
    code = jnp.where(parent >= 0, code, -1)
    rows = iota((4 * LANES, CAP), 0)
    select = (rows == code).astype(F32).astype(BF16)
    compress(leaves_ref, select, ff_both, filter_smem, work, level)
    leaves_ref[...] = leaves_ref[...] * keep_ref[...].astype(F32)
    parent = parent_two_ref[...]
    octant = octant_two_ref[...]
    local = parent - (origin >> 6)
    local = jnp.where(local < 0, 4, local)
    code = (octant >> 1) * LANES + (octant & 1) * 64 + local
    code = jnp.where(parent >= 0, code, -1)
    last = (octant[:, 0:1] + 7) & 7
    last = (last >> 1) * LANES + (last & 1) * 64 + 4
    code = jnp.concatenate([code, jnp.broadcast_to(last, (1, 32)), jnp.full((1, 64), -1, I32)], axis=1)
    rows = iota((4 * LANES, LANES), 0)
    lane = iota((4 * LANES, LANES), 1)
    select = ((rows == code) & (lane <= 32)).astype(F32).astype(BF16)
    compress(level, select, ff_both, filter_smem, work, level_up)
    one = turned(level, 40)
    two = turned(level_up, 8)
    one_ref[...] = one[:32]
    two_ref[...] = two[:4]
    send_ref[0:1, :] = one[32:33]
    send_ref[1:2, :] = two[4:5]


def finish_kernel(one_ref, two_ref, in_ref, parent_one_ref, parent_two_ref, one_out, two_out):
    for ref, parent_ref, out, n in ((one_ref, parent_one_ref, one_out, 0), (two_ref, parent_two_ref, two_out, 1)):
        rows = ref.shape[0]
        last = jnp.max(parent_ref[...], axis=1, keepdims=True) & (rows - 1)
        mask = (iota((rows, 1), 0) == last).astype(F32)
        out[...] = ref[...] + mask * in_ref[n : n + 1, :]


def column_table():
    table = np.full((8, 512), -1, np.int32)
    for n, e in enumerate(SAME_X):
        for j in range(K):
            for k in range(K):
                at = n * SQ + j * K + k
                table[0, at] = Y_CODE[e] * SQ + j
                table[1, at] = Z_CODE[e] * SQ + k
    return table


VMEM_SPEC = pl.BlockSpec(memory_space=pltpu.VMEM)
SMEM_SPEC = pl.BlockSpec(memory_space=pltpu.SMEM)
PARAMS = pltpu.CompilerParams(vmem_limit_bytes=63 * 1024 * 1024)


def shape(dims, dtype=F32):
    return jax.ShapeDtypeStruct(dims, dtype)


def edges(coeffs, neighbours):
    return pl.pallas_call(
        edges_kernel,
        out_shape=(shape((HALF, LANES)), shape((HALF, LANES))),
        in_specs=[VMEM_SPEC] * 2,
        out_specs=(VMEM_SPEC,) * 2,
        name="edges",
    )(coeffs, neighbours)


def operator_step(coeffs, from_left, from_right, terms, ints, filters):
    turned_filters = jnp.transpose(filters, (1, 0, 2))
    return pl.pallas_call(
        main_kernel,
        out_shape=(shape((KKK, CAP)), shape((32, KKK)), shape((4, KKK)), shape((2, KKK))),
        in_specs=[VMEM_SPEC] * 15 + [SMEM_SPEC],
        out_specs=(VMEM_SPEC,) * 4,
        scratch_shapes=[
            pltpu.VMEM((DENSE_ROWS, LANES), F32),
            pltpu.VMEM((2 * KT * LANES, LANES), F32),
            pltpu.VMEM((2, KT * LANES, LANES), BF16),
            pltpu.VMEM((2, KT * LANES, LANES), BF16),
            pltpu.VMEM((2 * HALF, LANES), F32),
            pltpu.VMEM((K, 16, 512), F32),
            pltpu.VMEM((K, 16, 512), F32),
            pltpu.VMEM((16, 1024), F32),
            pltpu.VMEM((KKK, LANES), F32),
            pltpu.VMEM((KKK, LANES), F32),
        ],
        compiler_params=PARAMS,
        name="operator",
    )(
        coeffs,
        from_left,
        from_right,
        *terms,
        *ints,
        jnp.asarray(column_table()),
        turned_filters,
        turned_filters,
    )


def finish(one, two, received, parent_one, parent_two):
    return pl.pallas_call(
        finish_kernel,
        out_shape=(shape((32, KKK)), shape((4, KKK))),
        in_specs=[VMEM_SPEC] * 5,
        out_specs=(VMEM_SPEC,) * 2,
        name="finish",
    )(one, two, received, parent_one, parent_two)


def per_device(
    coeffs, operator, filters, neighbours, parent_one, octant_one, parent_two, octant_two, keep
):
    terms = operator.reshape(3, 900)
    others = [
        lax.ppermute(terms, "rank", [(i, i ^ step) for i in range(4)]) for step in (1, 2, 3)
    ]
    to_chip, to_next = edges(coeffs, neighbours)
    count = lax.axis_size("box")
    pairs = [(i, i ^ 1) for i in range(count)]
    across = [(i, i + 1 if i % 2 else i - 1) for i in range(1, count - 1)]
    from_chip = lax.ppermute(to_chip, "box", pairs)
    from_next = lax.ppermute(to_next, "box", across)
    rows = [v[None] for v in (parent_one, octant_one, keep, parent_two, octant_two)]
    leaves, one, two, sent = operator_step(
        coeffs, from_chip, from_next, (terms, *others), (neighbours, *rows), filters
    )
    received = lax.ppermute(sent, "box", [(i + 1, i) for i in range(count - 1)])
    one, two = finish(one, two, received, rows[0], rows[3])
    return leaves, one.T, two.T


def solution(mesh):
    placed = (
        P(None, "box"),
        P("rank", None, None, None, None),
        P(),
        P(None, "box"),
        P("box"),
        P("box"),
        P("box"),
        P("box"),
        P("box"),
    )
    return jax.shard_map(
        per_device,
        mesh=mesh,
        in_specs=placed,
        out_specs=(P(None, "box"), P(None, "box"), P(None, "box")),
        check_vma=False,
    )
```
